32 devices in a mesh: guide: 2 (over core), tensor: 2 (over y), batch: 8 (over z, x).
Axes of the slice: x: 2, y: 2, z: 4, core: 2. Of those that a mesh axis runs over, the one named last changes fastest.
Arguments:
- latents: float32 [8, 16, 448], P('batch'), may hold values from -6 to 6
- lengths: int32 [8], P('batch'), may hold values from 1 to 448, 2240 in all
- timesteps: int32 [8], P('batch'), may hold values from 100 to 599
- guidance: float32 [8], P('batch'), may hold values from 1.5 to 6
- condition: float32 [2, 8, 1152], P('guide', 'batch'), may hold values from -6 to 6
- embed_weight: float32 [16, 1152], replicated, may hold values from -1.5 to 1.5
- modulation_weight: bfloat16 [2, 1152, 6, 1152], P(None, 'batch', None, 'tensor'), may hold values from -0.1875 to 0.1875
- final_modulation: bfloat16 [1152, 2, 1152], P('batch', None, 'tensor'), may hold values from -0.1875 to 0.1875
- qkv_weight: bfloat16 [2, 1152, 3, 1152], P(None, 'batch', None, 'tensor'), may hold values from -15 to 15
- proj_weight: bfloat16 [2, 1152, 1152], P(None, 'tensor', 'batch'), may hold values from -0.1875 to 0.1875
- up_weight: bfloat16 [2, 1152, 4608], P(None, 'batch', 'tensor'), may hold values from -0.1875 to 0.1875
- down_weight: bfloat16 [2, 4608, 1152], P(None, 'tensor', 'batch'), may hold values from -0.09375 to 0.09375
- output_weight: bfloat16 [1152, 16], replicated, may hold values from -0.1875 to 0.1875
Outputs:
- guided_noise: float32 [8, 16, 448], P('batch', 'guide', 'tensor')
- previous_latents: float32 [8, 16, 448], P('batch', 'guide', 'tensor')
The draws below stay inside these ranges and needn't reach their ends.
Inputs may be any that keep to these rules, and one draw needn't show every extreme that they name: `lengths`: at least one request has exactly 448 live tokens; all requests together have 8 * 448 * 5 // 8.
All inputs are finite; a program needn't handle non-finite values. No bound on the sum of `lengths` on one device may be relied on, other than what follows from the above.
Results may differ from the reference program's by a relative error of at most 0.025.
Values may be sent and summed in bfloat16 or wider, within the bound.
No kernel may reach another device: no remote copies, remote signals or barrier semaphores. Data moves between devices by JAX's collectives and lax.ppermute only.
A program may use at most 128 MiB of HBM per device.

```python
import math
import jax
import jax.numpy as jnp
import numpy as np
from jax import lax

D = 1152
HEADS = 16
HDIM = 72
FF = 4608
PATCH = 16
LAYERS = 2
MAXLEN = 448
TRAIN_STEPS = 1000
STRIDE = 20
REQUESTS = 8
N_TENSOR = 2


def draw_qkv_weight(key, part):
    normal_part = jnp.clip(jax.random.normal(key, (LAYERS, D, 3, D), jnp.float32), -5.0, 5.0) * (1.0 / math.sqrt(D))
    return jnp.clip(normal_part, -15.0, 15.0).astype(jnp.bfloat16)


def with_ends(entries, key, low, top_value):
    shape = entries.shape
    spot = [jax.random.randint(jax.random.fold_in(key, axis), (), 0, shape[axis]) for axis in range(len(shape))]
    entries = entries.at[tuple(spot)].set(low)
    longest = shape.index(max(shape))
    spot[longest] = (spot[longest] + 1) % shape[longest]
    return entries.at[tuple(spot)].set(top_value)


def level_of(key, shape, shards, low, largest):
    gain = 1.0
    for axis_at, parts in shards:
        heights = jax.random.uniform(jax.random.fold_in(jax.random.fold_in(key, 6), axis_at), (parts,), jnp.float32, low / len(shards), largest / len(shards))
        gain = gain * jnp.repeat(jnp.exp(heights), shape[axis_at] // parts).reshape((-1,) + (1,) * (len(shape) - 1 - axis_at))
    return gain


def split_up(number_of, total, limit, lean):
    portions = [(1 << 20) // math.isqrt(rank ** lean) + 1 for rank in range(2, number_of + 1)]
    surplus, counts = total - limit - (number_of - 1), [1] * (number_of - 1)
    while surplus > 0:
        free = [i for i in range(number_of - 1) if counts[i] < limit]
        mass, remaining = sum([portions[i] for i in free]), surplus
        for i in free:
            more = min(limit - counts[i], max(1, remaining * portions[i] // mass), surplus)
            counts[i] = counts[i] + more
            surplus = surplus - more
    return np.array([limit] + counts)


def uneven_parts(key, amount, total, most, skew):
    if amount == 2:
        one = jax.random.randint(key, (), max(1, total - most), min(most, total - 1) + 1)
        return jnp.stack([one, total - one])
    sizes = jnp.asarray(split_up(amount, total, most, skew), jnp.int32)
    pairs = (amount - 1) // 2
    donor, receiver = sizes[1:1 + 2 * pairs:2], sizes[2:2 + 2 * pairs:2]
    slack = jnp.minimum(donor - 1, most - receiver)
    moved = jax.random.randint(jax.random.fold_in(key, 1), (pairs,), 0, 1 << 20) % (slack + 1)
    sizes = sizes.at[1:1 + 2 * pairs:2].set(donor - moved).at[2:2 + 2 * pairs:2].set(receiver + moved)
    return sizes[jax.random.permutation(jax.random.fold_in(key, 2), amount)]


def normal_values(stream_key, shape, scale, most, shards=(), kind=jnp.bfloat16):
    array = scale * jax.random.normal(stream_key, shape, jnp.float32)
    if shards:
        array = array * level_of(stream_key, shape, shards, -0.22, 0.18)
    return jnp.clip(array, -most, most).astype(kind)


def setup_inputs(seed: int = 0) -> dict:
    key_of = jax.random.split(jax.random.key(seed), 14)
    return {
        "latents": normal_values(key_of[0], (REQUESTS, PATCH, MAXLEN), 1.0, 6.0, ((0, 8),), jnp.float32),
        "lengths": uneven_parts(key_of[1], REQUESTS, REQUESTS * MAXLEN * 5 // 8, MAXLEN, 2).astype(jnp.int32),
        "timesteps": with_ends(jax.random.randint(key_of[2], (REQUESTS,), 100, 600), jax.random.fold_in(key_of[2], 1), 100, 599).astype(jnp.int32),
        "guidance": jnp.clip(1.5 + 4.5 * jax.random.uniform(key_of[3], (REQUESTS,), jnp.float32) ** level_of(key_of[3], (REQUESTS,), ((0, 8),), -0.2, 0.2), 1.5, 6.0),
        "condition": normal_values(key_of[4], (2, REQUESTS, D), 1.0, 6.0, ((0, 2), (1, 8)), jnp.float32),
        "embed_weight": normal_values(key_of[5], (PATCH, D), PATCH ** -0.5, 1.5, (), jnp.float32),
        "modulation_weight": normal_values(key_of[6], (LAYERS, D, 6, D), D ** -0.5, 0.1875, ((1, 8), (3, 2))),
        "final_modulation": normal_values(key_of[7], (D, 2, D), D ** -0.5, 0.1875, ((0, 8), (2, 2))),
        "qkv_weight": draw_qkv_weight(jax.random.fold_in(key_of[13], 71), 0),
        "proj_weight": normal_values(key_of[9], (LAYERS, D, D), D ** -0.5, 0.1875, ((1, 2), (2, 8))),
        "up_weight": normal_values(key_of[10], (LAYERS, D, FF), D ** -0.5, 0.1875, ((1, 8), (2, 2))),
        "down_weight": normal_values(key_of[11], (LAYERS, FF, D), FF ** -0.5, 0.09375, ((1, 2), (2, 8))),
        "output_weight": normal_values(key_of[12], (D, PATCH), D ** -0.5, 0.1875),
    }


norm_epsilon = 1e-06

def wide_dot(left, right):
    return jnp.dot(left.astype(jnp.float32), right.astype(jnp.float32), precision=lax.Precision.HIGHEST)

def layer_norm(values):
    center = values - lax.optimization_barrier(jnp.mean(values, axis=-1, keepdims=True))
    spread = lax.optimization_barrier(jnp.mean(center * center, axis=-1, keepdims=True))
    return center * lax.rsqrt(spread + norm_epsilon)

def modulate(values, shift, scale):
    return layer_norm(values) * (1.0 + scale) + shift

def position_table(first_row, row_count, width):
    rows_at = (first_row + jnp.arange(row_count, dtype=jnp.int32)).astype(jnp.float32)
    half_width = width // 2
    frequency = jnp.exp(jnp.arange(half_width, dtype=jnp.float32) * (-math.log(10000.0) / half_width))
    angles = rows_at[:, None] * frequency[None, :]
    return jnp.concatenate([jnp.sin(angles), jnp.cos(angles)], axis=1)

def grouped_product(activation, weight_mat):
    row_count, inner_count = activation.shape
    pieces = activation.reshape(row_count, N_TENSOR, inner_count // N_TENSOR).astype(jnp.float32)
    blocks = weight_mat.reshape(N_TENSOR, inner_count // N_TENSOR, weight_mat.shape[1]).astype(jnp.float32)
    partial_terms = jnp.einsum('lgk,gkd->gld', pieces, blocks, precision=lax.Precision.HIGHEST).astype(jnp.bfloat16)
    return lax.optimization_barrier(jnp.sum(partial_terms.astype(jnp.float32), axis=0))

def reference(latents, lengths, timesteps, guidance, condition, embed_weight, modulation_weight, final_modulation, qkv_weight, proj_weight, up_weight, down_weight, output_weight):
    cond_act = jax.nn.silu(condition).astype(jnp.bfloat16).reshape(2 * REQUESTS, D)
    block_flat = jnp.transpose(modulation_weight, (1, 0, 2, 3)).reshape(D, LAYERS * 6 * D)
    block_mods = wide_dot(cond_act, block_flat).reshape(2 * REQUESTS, LAYERS, 6, D)
    final_mods = wide_dot(cond_act, final_modulation.reshape(D, 2 * D)).reshape(2 * REQUESTS, 2, D)
    positions = jnp.arange(MAXLEN, dtype=jnp.int32)
    live_mask = positions[None, :] < lengths[:, None]
    positional = position_table(0, MAXLEN, D)
    score_scale = 1.0 / math.sqrt(HDIM)

    def run_item(operands):
        latent_item, item_block, item_final, key_live = operands
        hidden_state = jnp.einsum('pl,pd->ld', latent_item, embed_weight, precision=lax.Precision.HIGHEST) + positional
        for layer_at in range(LAYERS):
            modulation = item_block[layer_at]
            normed = modulate(hidden_state, modulation[0], modulation[1]).astype(jnp.bfloat16)
            projected = wide_dot(normed, qkv_weight[layer_at].reshape(D, 3 * D)).astype(jnp.bfloat16)
            projected = projected.reshape(MAXLEN, 3, HEADS, HDIM).astype(jnp.float32)
            scores = jnp.einsum('qhd,khd->hqk', projected[:, 0], projected[:, 1], precision=lax.Precision.HIGHEST) * score_scale
            scores = jnp.where(key_live[None, None, :], scores, -jnp.inf)
            row_max = lax.optimization_barrier(jnp.max(scores, axis=-1, keepdims=True))
            exp_scores = jnp.exp(scores - row_max)
            probabilities = (exp_scores / lax.optimization_barrier(jnp.sum(exp_scores, axis=-1, keepdims=True))).astype(jnp.bfloat16)
            attended = jnp.einsum('hqk,khd->qhd', probabilities.astype(jnp.float32), projected[:, 2], precision=lax.Precision.HIGHEST).astype(jnp.bfloat16).reshape(MAXLEN, D)
            hidden_state = hidden_state + modulation[2] * grouped_product(attended, proj_weight[layer_at])
            normed = modulate(hidden_state, modulation[3], modulation[4]).astype(jnp.bfloat16)
            hidden_units = jax.nn.gelu(wide_dot(normed, up_weight[layer_at]), approximate=True).astype(jnp.bfloat16)
            hidden_state = hidden_state + modulation[5] * grouped_product(hidden_units, down_weight[layer_at])
        final_in = modulate(hidden_state, item_final[0], item_final[1]).astype(jnp.bfloat16)
        return wide_dot(final_in, output_weight).T
    latent_items = jnp.concatenate([latents, latents], axis=0)
    live_items = jnp.concatenate([live_mask, live_mask], axis=0)
    noise_all = lax.map(run_item, (latent_items, block_mods, final_mods, live_items)).reshape(2, REQUESTS, PATCH, MAXLEN)
    beta_values = jnp.linspace(0.0001, 0.02, TRAIN_STEPS, dtype=jnp.float32)
    alpha_bar = jnp.cumprod(1.0 - beta_values)
    alpha_now = alpha_bar[timesteps][:, None, None]
    alpha_prev = alpha_bar[timesteps - STRIDE][:, None, None]
    cond_noise = noise_all[0]
    uncond_noise = noise_all[1]
    live_out = live_mask[:, None, :]
    guided = uncond_noise + guidance[:, None, None] * (cond_noise - uncond_noise)
    guided = jnp.where(live_out, guided, 0.0)
    start_est = (latents - jnp.sqrt(1.0 - alpha_now) * guided) / jnp.sqrt(alpha_now)
    previous = jnp.sqrt(alpha_prev) * start_est + jnp.sqrt(1.0 - alpha_prev) * guided
    previous = jnp.where(live_out, previous, 0.0)
    return (guided, previous)
```

```python
import functools
import math

import jax
import jax.numpy as jnp
import numpy as np
from jax import lax
from jax.experimental import pallas as pl
from jax.experimental.pallas import tpu as pltpu
from jax.sharding import PartitionSpec as P

HDIM = 72
TRAIN_STEPS = 1000
STRIDE = 20


norm_epsilon = 1e-06


def from_partner(block, axis, distance):
    count = lax.axis_size(axis)
    route = []
    for low in range(count):
        high = low | 1 << distance
        if high != low and high < count:
            route += [(low, high), (high, low)]
    return lax.ppermute(block, axis, route)


def layer_norm(values):
    center = values - jnp.mean(values, axis=-1, keepdims=True)
    spread = jnp.mean(center * center, axis=-1, keepdims=True)
    return center * lax.rsqrt(spread + norm_epsilon)


def modulate(values, shift, scale):
    return layer_norm(values) * (1.0 + scale[:, None, :]) + shift[:, None, :]


def position_table(row_count, width):
    rows_at = jnp.arange(row_count, dtype=jnp.int32).astype(jnp.float32)
    half_width = width // 2
    frequency = jnp.exp(
        jnp.arange(half_width, dtype=jnp.float32) * (-math.log(10000.0) / half_width)
    )
    angles = rows_at[:, None] * frequency[None, :]
    return jnp.concatenate([jnp.sin(angles), jnp.cos(angles)], axis=1)


def attend(operands):
    projected_item, key_live = operands
    score_scale = 1.0 / math.sqrt(HDIM)
    scores = (
        jnp.einsum(
            "qhd,khd->hqk",
            projected_item[:, 0],
            projected_item[:, 1],
            preferred_element_type=jnp.float32,
        )
        * score_scale
    )
    scores = jnp.where(key_live[None, None, :], scores, -jnp.inf)
    row_max = jnp.max(scores, axis=-1, keepdims=True)
    exp_scores = jnp.exp(scores - row_max)
    probabilities = (exp_scores / jnp.sum(exp_scores, axis=-1, keepdims=True)).astype(jnp.bfloat16)
    attended = jnp.einsum(
        "hqk,khd->qhd", probabilities, projected_item[:, 2], preferred_element_type=jnp.float32
    )
    return attended.astype(jnp.bfloat16).reshape(
        attended.shape[0], attended.shape[1] * attended.shape[2]
    )


def local(
    latents,
    lengths,
    timesteps,
    guidance,
    condition,
    embed_weight,
    modulation_weight,
    final_modulation,
    qkv_weight,
    proj_weight,
    up_weight,
    down_weight,
    output_weight,
):
    tensor_count = lax.axis_size("tensor")
    batch_count = lax.axis_size("batch")
    tensor_at = lax.axis_index("tensor")
    batch_at = lax.axis_index("batch")
    req_local, patch_size, max_len = latents.shape
    width = embed_weight.shape[1]
    layer_count = qkv_weight.shape[0]
    head_cols = qkv_weight.shape[3]
    heads_local = head_cols // HDIM
    rows_local = max_len // tensor_count
    width_piece = width // batch_count
    mod_count = 6 * layer_count + 2

    def rows_product(activation, shard):
        return jnp.dot(
            activation,
            lax.all_gather(shard, "batch", axis=0, tiled=True),
            preferred_element_type=jnp.float32,
        )

    def cols_product(activation, shard):
        return jnp.dot(
            activation,
            lax.all_gather(shard, "batch", axis=1, tiled=True),
            preferred_element_type=jnp.float32,
        )

    cond_act = jax.nn.silu(condition[0]).astype(jnp.bfloat16)
    cond_all = lax.all_gather(cond_act, "batch", axis=0, tiled=True)
    cond_cols = lax.dynamic_slice_in_dim(cond_all, batch_at * width_piece, width_piece, 1)
    block_local = jnp.transpose(modulation_weight, (1, 0, 2, 3)).reshape(
        width_piece, 6 * layer_count * head_cols
    )
    mod_local = jnp.concatenate(
        [block_local, final_modulation.reshape(width_piece, 2 * head_cols)], axis=1
    )
    mod_mine = lax.psum_scatter(
        jnp.dot(cond_cols, mod_local, preferred_element_type=jnp.float32),
        "batch",
        scatter_dimension=0,
        tiled=True,
    )
    mod_full = lax.all_gather(
        mod_mine.reshape(req_local, mod_count, head_cols), "tensor", axis=2, tiled=True
    )
    positions = jnp.arange(max_len, dtype=jnp.int32)
    live_mask = positions[None, :] < lengths[:, None]
    own_start = tensor_at * rows_local
    hidden_state = (
        jnp.einsum("rpl,pd->rld", latents, embed_weight, precision=lax.Precision.HIGHEST)
        + position_table(max_len, width)[None]
    )
    for layer_at in range(layer_count):
        modulation = mod_full[:, 6 * layer_at : 6 * layer_at + 6]
        normed = modulate(hidden_state, modulation[:, 0], modulation[:, 1]).astype(jnp.bfloat16)
        projected = rows_product(
            normed.reshape(req_local * max_len, width),
            qkv_weight[layer_at].reshape(width_piece, 3 * head_cols),
        ).astype(jnp.bfloat16)
        projected = projected.reshape(req_local, max_len, 3, heads_local, HDIM)
        attended = lax.map(attend, (projected, live_mask))
        branch = cols_product(
            attended.reshape(req_local * max_len, head_cols), proj_weight[layer_at]
        ).reshape(req_local, max_len, width)
        branch = lax.psum(branch.astype(jnp.bfloat16), "tensor").astype(jnp.float32)
        hidden_state = hidden_state + modulation[:, 2][:, None, :] * branch
        normed = modulate(hidden_state, modulation[:, 3], modulation[:, 4]).astype(jnp.bfloat16)
        hidden_units = jax.nn.gelu(
            rows_product(normed.reshape(req_local * max_len, width), up_weight[layer_at]),
            approximate=True,
        ).astype(jnp.bfloat16)
        branch = cols_product(hidden_units, down_weight[layer_at]).reshape(
            req_local, max_len, width
        )
        branch = lax.psum(branch.astype(jnp.bfloat16), "tensor").astype(jnp.float32)
        hidden_state = hidden_state + modulation[:, 5][:, None, :] * branch
    hidden_state = lax.dynamic_slice_in_dim(hidden_state, own_start, rows_local, 1)
    final_in = modulate(
        hidden_state, mod_full[:, 6 * layer_count], mod_full[:, 6 * layer_count + 1]
    ).astype(jnp.bfloat16)
    noise_own = jnp.einsum(
        "rld,dp->rpl", final_in, output_weight, preferred_element_type=jnp.float32
    )
    return finish(latents, lengths, timesteps, guidance, noise_own, rows_local)


def alpha_table():
    beta_values = np.linspace(0.0001, 0.02, TRAIN_STEPS, dtype=np.float32)
    return np.cumprod(np.float32(1.0) - beta_values, dtype=np.float32)


def finish(latents, lengths, timesteps, guidance, noise_own, rows_local):
    patch_size, max_len = latents.shape[1:]
    guide_at = lax.axis_index("guide")
    is_first = guide_at == 0
    own_start = lax.axis_index("tensor") * rows_local
    own_latents = lax.dynamic_slice_in_dim(latents, own_start, rows_local, 2)
    own_live = (own_start + jnp.arange(rows_local, dtype=jnp.int32))[None, :] < lengths[:, None]
    half_patch = patch_size // 2
    mine_noise = lax.dynamic_slice_in_dim(noise_own, guide_at * half_patch, half_patch, 1)
    other_noise = lax.dynamic_slice_in_dim(noise_own, (1 - guide_at) * half_patch, half_patch, 1)
    partner_noise = from_partner(other_noise, "guide", 0)
    cond_noise = jnp.where(is_first, mine_noise, partner_noise)
    uncond_noise = jnp.where(is_first, partner_noise, mine_noise)
    live_out = own_live[:, None, :]
    guided = uncond_noise + guidance[:, None, None] * (cond_noise - uncond_noise)
    guided = jnp.where(live_out, guided, 0.0)
    half_latents = lax.dynamic_slice_in_dim(own_latents, guide_at * half_patch, half_patch, 1)
    alpha_bar = jnp.asarray(alpha_table())
    step_ids = jnp.arange(TRAIN_STEPS, dtype=jnp.int32)
    alpha_now = jnp.sum(
        jnp.where(step_ids[None, :] == timesteps[:, None], alpha_bar[None, :], 0.0), axis=1
    )[:, None, None]
    alpha_prev = jnp.sum(
        jnp.where(step_ids[None, :] == (timesteps - STRIDE)[:, None], alpha_bar[None, :], 0.0),
        axis=1,
    )[:, None, None]
    start_est = (half_latents - jnp.sqrt(1.0 - alpha_now) * guided) / jnp.sqrt(alpha_now)
    previous = jnp.sqrt(alpha_prev) * start_est + jnp.sqrt(1.0 - alpha_prev) * guided
    previous = jnp.where(live_out, previous, 0.0)
    return (guided, previous)


BATCH_BITS = (4, 2, 1)


def exchange(block, axis, bit):
    count = lax.axis_size(axis)
    return lax.ppermute(block, axis, [(at, at ^ bit) for at in range(count)])


def gather_piece(own, bits):
    held, distances = own, [0]
    for bit in bits[:-1]:
        held = jnp.concatenate([held, exchange(held, "batch", bit)], axis=0)
        distances = distances + [at ^ bit for at in distances]
    last = bits[-1]
    far = exchange(held, "batch", last)
    buffers = [held, far, exchange(held, "guide", 1), exchange(far, "guide", 1)]
    return buffers, [distances, [at ^ last for at in distances]]


def place(weights, slots, buffers, distances, batch_at):
    rows = buffers[0].shape[0] // 4
    for which, buffer in enumerate(buffers):
        for at in range(4):
            row = pl.multiple_of((batch_at ^ distances[which % 2][at]) * rows, 16)
            weights[slots[which // 2], pl.ds(row, rows), :] = buffer[at * rows : (at + 1) * rows, :]


def normalized(hidden, shift, scale):
    center = hidden - jnp.mean(hidden, axis=-1, keepdims=True)
    spread = jnp.mean(center * center, axis=-1, keepdims=True)
    return center * lax.rsqrt(spread + norm_epsilon) * (1.0 + scale) + shift


def dot_nt(left, right):
    return lax.dot_general(
        left, right, (((1,), (1,)), ((), ())), preferred_element_type=jnp.float32
    )


def kernel_call(body, outs, scratch, operands, flops, bytes_moved, grid_free=True):
    specs = [pl.BlockSpec(memory_space=pltpu.SMEM)] + [
        pl.BlockSpec(memory_space=pltpu.VMEM) for _ in operands[1:]
    ]
    return pl.pallas_call(
        body,
        out_shape=outs,
        in_specs=specs,
        out_specs=jax.tree.map(lambda _: pl.BlockSpec(memory_space=pltpu.VMEM), outs),
        scratch_shapes=scratch,
        cost_estimate=pl.CostEstimate(
            flops=int(flops), bytes_accessed=int(bytes_moved), transcendentals=0
        ),
        compiler_params=pltpu.CompilerParams(vmem_limit_bytes=44 * 2**20),
    )(*operands)


def residual(hidden, branches, mods, gate_row):
    if not branches:
        return hidden[...]
    total = branches[0][...].astype(jnp.float32) + branches[1][...].astype(jnp.float32)
    return hidden[...] + mods[gate_row : gate_row + 1, :] * total


def qkv_kernel(distances, layer, heads, with_branch, ids, hidden, mods, *refs):
    branches, refs = (refs[:2], refs[2:]) if with_branch else ((), refs)
    buffers, refs = refs[:4], refs[4:]
    if with_branch:
        hidden_out, refs = refs[0], refs[1:]
    heads_out, proj_out, weights, normed, projected = refs
    width = hidden.shape[1]
    half = width // 2
    place(weights, [ids[1], 1 - ids[1]], buffers, distances, ids[0])
    state = residual(hidden, branches, mods, 6 * layer - 1)
    if with_branch:
        hidden_out[...] = state
    row = 6 * layer
    normed[...] = normalized(state, mods[row : row + 1, :], mods[row + 1 : row + 2, :]).astype(
        jnp.bfloat16
    )
    proj_out[...] = weights[1, :, half:]

    def step(at, carry):
        lo = pl.multiple_of(at * 384, 128)
        projected[:, pl.ds(lo, 384)] = jnp.dot(
            normed[...], weights[0, :, pl.ds(lo, 384)], preferred_element_type=jnp.float32
        ).astype(jnp.bfloat16)
        return carry

    lax.fori_loop(0, width // 384, step, 0)
    projected[:, width:] = jnp.dot(
        normed[...], weights[1, :, :half], preferred_element_type=jnp.float32
    ).astype(jnp.bfloat16)
    for at in range(3 * heads):
        heads_out[at] = projected[:, at * HDIM : (at + 1) * HDIM]


def attention_kernel(first_row, heads, ids, heads_in, proj, partial, attended):
    rows = partial.shape[0]
    keys = heads_in.shape[1]
    factor = math.log2(math.e) / math.sqrt(HDIM)
    live = lax.broadcasted_iota(jnp.int32, (1, keys), 1) < ids[3]
    for at in range(heads):
        scores = dot_nt(heads_in[at, first_row : first_row + rows, :], heads_in[heads + at])
        scores = jnp.where(live, scores * factor, -jnp.inf)
        raised = jnp.exp2(scores - jnp.max(scores, axis=-1, keepdims=True))
        total = jnp.sum(raised, axis=-1, keepdims=True)
        out = jnp.dot(
            raised.astype(jnp.bfloat16), heads_in[2 * heads + at], preferred_element_type=jnp.float32
        )
        attended[:, at * HDIM : (at + 1) * HDIM] = (out / total).astype(jnp.bfloat16)
    partial[...] = dot_nt(attended[...], proj[...]).astype(jnp.bfloat16)


def up_kernel(distances, layer, ids, hidden, mods, *refs):
    branches, refs = refs[:2], refs[2:]
    buffers, refs = refs[:4], refs[4:]
    hidden_out, units, weights, normed = refs
    width = hidden.shape[1]
    place(weights, [0, 1], buffers, distances, ids[0])
    state = residual(hidden, branches, mods, 6 * layer + 2)
    hidden_out[...] = state
    row = 6 * layer + 3
    normed[...] = normalized(state, mods[row : row + 1, :], mods[row + 1 : row + 2, :]).astype(
        jnp.bfloat16
    )
    for half in range(2):

        def step(at, carry):
            lo = pl.multiple_of(at * 384, 128)
            product = jnp.dot(
                normed[...], weights[half, :, pl.ds(lo, 384)], preferred_element_type=jnp.float32
            )
            inner = math.sqrt(2.0 / math.pi) * (product + 0.044715 * product * product * product)
            units[half, :, pl.ds(lo, 384)] = (0.5 * product * (1.0 + jnp.tanh(inner))).astype(
                jnp.bfloat16
            )
            return carry

        lax.fori_loop(0, width // 384, step, 0)


def down_kernel(distances, ids, units, *refs):
    buffers, (partial, weights) = refs[:4], refs[4:]
    width = partial.shape[1]
    place(weights, [0, 1], buffers, distances, ids[0])

    def step(at, carry):
        lo = pl.multiple_of(at * 384, 128)
        product = dot_nt(units[0], weights[0, pl.ds(lo, 384), :])
        product = product + dot_nt(units[1], weights[1, pl.ds(lo, 384), :])
        partial[:, pl.ds(lo, 384)] = product.astype(jnp.bfloat16)
        return carry

    lax.fori_loop(0, width // 384, step, 0)


def modulations(condition, modulation_weight, final_modulation):
    layer_count, width_piece, _, head_cols = modulation_weight.shape
    count = 6 * layer_count + 2
    batch_at = lax.axis_index("batch")
    gathered = jax.nn.silu(condition[0]).astype(jnp.bfloat16)
    for bit in BATCH_BITS:
        gathered = jnp.concatenate([gathered, exchange(gathered, "batch", bit)], axis=0)
    columns = lax.dynamic_slice_in_dim(gathered, batch_at * width_piece, width_piece, 1)
    blocks = jnp.einsum(
        "rk,lkjc->rljc", columns, modulation_weight, preferred_element_type=jnp.float32
    ).reshape(columns.shape[0], 6 * layer_count, head_cols)
    finals = jnp.einsum("rk,kjc->rjc", columns, final_modulation, preferred_element_type=jnp.float32)
    sums = jnp.concatenate([blocks, finals], axis=1)
    for bit in reversed(BATCH_BITS):
        keep = sums.shape[0] // 2
        sums = sums[:keep] + exchange(sums[keep:], "batch", bit)
    mine = sums[0]
    other = exchange(mine, "tensor", 1)
    first = lax.axis_index("tensor") == 0
    return jnp.concatenate(
        [jnp.where(first, mine, other), jnp.where(first, other, mine)], axis=1
    )


def fast_local(
    latents,
    lengths,
    timesteps,
    guidance,
    condition,
    embed_weight,
    modulation_weight,
    final_modulation,
    qkv_weight,
    proj_weight,
    up_weight,
    down_weight,
    output_weight,
):
    tensor_at = lax.axis_index("tensor")
    batch_at = lax.axis_index("batch")
    guide_at = lax.axis_index("guide")
    _, patch_size, max_len = latents.shape
    width = embed_weight.shape[1]
    half = width // 2
    layer_count = qkv_weight.shape[0]
    heads = half // HDIM
    rows_own = max_len // 2
    width_piece = qkv_weight.shape[1]
    first = guide_at == 0
    ids = jnp.stack([batch_at, guide_at, tensor_at, lengths[0]]).astype(jnp.int32)
    bf16, f32 = jnp.bfloat16, jnp.float32

    def attention_piece(layer):
        queries_keys = qkv_weight[layer, :, :2].reshape(width_piece, width)
        values_proj = jnp.concatenate([qkv_weight[layer, :, 2], proj_weight[layer].T], axis=1)
        return jnp.where(first, queries_keys, values_proj)

    pieces = []
    for layer in range(layer_count):
        pieces.append(gather_piece(attention_piece(layer), (4, 2, 1)))
        pieces.append(
            gather_piece(
                lax.dynamic_slice_in_dim(up_weight[layer], guide_at * width, width, 1), (4, 2, 1)
            )
        )
        pieces.append(
            gather_piece(
                lax.dynamic_slice_in_dim(down_weight[layer], guide_at * width, width, 0).T, (4, 2, 1)
            )
        )
    mods = modulations(condition, modulation_weight, final_modulation)
    hidden = jnp.einsum(
        "pl,pd->ld", latents[0], embed_weight, precision=lax.Precision.HIGHEST
    ) + position_table(max_len, width)

    weight_bytes = 4 * width * width
    shape = jax.ShapeDtypeStruct
    two_weights = pltpu.VMEM((2, width, width), bf16)
    normed = pltpu.VMEM((max_len, width), bf16)
    branches = []
    for layer in range(layer_count):
        buffers, distances = pieces[3 * layer]
        with_branch = layer > 0
        outs = [shape((3 * heads, max_len, HDIM), bf16), shape((width, half), bf16)]
        if with_branch:
            outs = [shape((max_len, width), f32)] + outs
        results = kernel_call(
            functools.partial(qkv_kernel, distances, layer, heads, with_branch),
            outs,
            [two_weights, normed, pltpu.VMEM((max_len, 3 * half), bf16)],
            [ids, hidden, mods, *branches, *buffers],
            2 * max_len * width * 3 * half,
            weight_bytes,
        )
        if with_branch:
            hidden = results[0]
        projected, proj_full = results[-2:]
        parts = [
            kernel_call(
                functools.partial(attention_kernel, at * rows_own, heads),
                shape((rows_own, width), bf16),
                [pltpu.VMEM((rows_own, half), bf16)],
                [ids, projected, proj_full],
                4 * rows_own * max_len * half + 2 * rows_own * half * width,
                weight_bytes,
            )
            for at in range(2)
        ]
        received = [exchange(part, "tensor", 1) for part in parts]
        branches = [jnp.concatenate(parts, axis=0), jnp.concatenate(received, axis=0)]
        buffers, distances = pieces[3 * layer + 1]
        hidden, units = kernel_call(
            functools.partial(up_kernel, distances, layer),
            [shape((max_len, width), f32), shape((2, max_len, width), bf16)],
            [two_weights, normed],
            [ids, hidden, mods, *branches, *buffers],
            4 * max_len * width * width,
            weight_bytes,
        )
        buffers, distances = pieces[3 * layer + 2]
        partial = kernel_call(
            functools.partial(down_kernel, distances),
            shape((max_len, width), bf16),
            [two_weights],
            [ids, units, *buffers],
            4 * max_len * width * width,
            weight_bytes,
        )
        if layer + 1 < layer_count:
            branches = [partial, exchange(partial, "tensor", 1)]
    own_start = tensor_at * rows_own
    mine = lax.dynamic_slice_in_dim(partial, own_start, rows_own, 0)
    theirs = exchange(
        lax.dynamic_slice_in_dim(partial, (1 - tensor_at) * rows_own, rows_own, 0), "tensor", 1
    )
    hidden = lax.dynamic_slice_in_dim(hidden, own_start, rows_own, 0)
    hidden = hidden + mods[6 * layer_count - 1][None, :] * (
        mine.astype(f32) + theirs.astype(f32)
    )
    final_in = normalized(
        hidden, mods[6 * layer_count][None, :], mods[6 * layer_count + 1][None, :]
    ).astype(bf16)
    noise_own = lax.dot_general(
        output_weight, final_in, (((0,), (1,)), ((), ())), preferred_element_type=f32
    )[None]
    return finish(latents, lengths, timesteps, guidance, noise_own, rows_own)


def solution(mesh):
    in_specs = (
        P("batch", None, None),
        P("batch"),
        P("batch"),
        P("batch"),
        P("guide", "batch", None),
        P(),
        P(None, "batch", None, "tensor"),
        P("batch", None, "tensor"),
        P(None, "batch", None, "tensor"),
        P(None, "tensor", "batch"),
        P(None, "batch", "tensor"),
        P(None, "tensor", "batch"),
        P(),
    )
    out_specs = (P("batch", "guide", "tensor"), P("batch", "guide", "tensor"))
    sizes = mesh.shape
    small = sizes["batch"] == 8 and sizes["tensor"] == 2
    body = fast_local if small else local
    return jax.shard_map(body, mesh=mesh, in_specs=in_specs, out_specs=out_specs, check_vma=False)
```

```python
import functools
import math

import jax
import jax.numpy as jnp
import numpy as np
from jax import lax
from jax.experimental import pallas as pl
from jax.experimental.pallas import tpu as pltpu
from jax.sharding import PartitionSpec as P

HDIM = 72
TRAIN_STEPS = 1000
STRIDE = 20


norm_epsilon = 1e-06


def from_partner(block, axis, distance):
    count = lax.axis_size(axis)
    route = []
    for low in range(count):
        high = low | 1 << distance
        if high != low and high < count:
            route += [(low, high), (high, low)]
    return lax.ppermute(block, axis, route)


def layer_norm(values):
    center = values - jnp.mean(values, axis=-1, keepdims=True)
    spread = jnp.mean(center * center, axis=-1, keepdims=True)
    return center * lax.rsqrt(spread + norm_epsilon)


def modulate(values, shift, scale):
    return layer_norm(values) * (1.0 + scale[:, None, :]) + shift[:, None, :]


def position_table(row_count, width):
    rows_at = jnp.arange(row_count, dtype=jnp.int32).astype(jnp.float32)
    half_width = width // 2
    frequency = jnp.exp(
        jnp.arange(half_width, dtype=jnp.float32) * (-math.log(10000.0) / half_width)
    )
    angles = rows_at[:, None] * frequency[None, :]
    return jnp.concatenate([jnp.sin(angles), jnp.cos(angles)], axis=1)


def attend(operands):
    projected_item, key_live = operands
    score_scale = 1.0 / math.sqrt(HDIM)
    scores = (
        jnp.einsum(
            "qhd,khd->hqk",
            projected_item[:, 0],
            projected_item[:, 1],
            preferred_element_type=jnp.float32,
        )
        * score_scale
    )
    scores = jnp.where(key_live[None, None, :], scores, -jnp.inf)
    row_max = jnp.max(scores, axis=-1, keepdims=True)
    exp_scores = jnp.exp(scores - row_max)
    probabilities = (exp_scores / jnp.sum(exp_scores, axis=-1, keepdims=True)).astype(jnp.bfloat16)
    attended = jnp.einsum(
        "hqk,khd->qhd", probabilities, projected_item[:, 2], preferred_element_type=jnp.float32
    )
    return attended.astype(jnp.bfloat16).reshape(
        attended.shape[0], attended.shape[1] * attended.shape[2]
    )


def local(
    latents,
    lengths,
    timesteps,
    guidance,
    condition,
    embed_weight,
    modulation_weight,
    final_modulation,
    qkv_weight,
    proj_weight,
    up_weight,
    down_weight,
    output_weight,
):
    tensor_count = lax.axis_size("tensor")
    batch_count = lax.axis_size("batch")
    tensor_at = lax.axis_index("tensor")
    batch_at = lax.axis_index("batch")
    req_local, patch_size, max_len = latents.shape
    width = embed_weight.shape[1]
    layer_count = qkv_weight.shape[0]
    head_cols = qkv_weight.shape[3]
    heads_local = head_cols // HDIM
    rows_local = max_len // tensor_count
    width_piece = width // batch_count
    mod_count = 6 * layer_count + 2

    def rows_product(activation, shard):
        return jnp.dot(
            activation,
            lax.all_gather(shard, "batch", axis=0, tiled=True),
            preferred_element_type=jnp.float32,
        )

    def cols_product(activation, shard):
        return jnp.dot(
            activation,
            lax.all_gather(shard, "batch", axis=1, tiled=True),
            preferred_element_type=jnp.float32,
        )

    cond_act = jax.nn.silu(condition[0]).astype(jnp.bfloat16)
    cond_all = lax.all_gather(cond_act, "batch", axis=0, tiled=True)
    cond_cols = lax.dynamic_slice_in_dim(cond_all, batch_at * width_piece, width_piece, 1)
    block_local = jnp.transpose(modulation_weight, (1, 0, 2, 3)).reshape(
        width_piece, 6 * layer_count * head_cols
    )
    mod_local = jnp.concatenate(
        [block_local, final_modulation.reshape(width_piece, 2 * head_cols)], axis=1
    )
    mod_mine = lax.psum_scatter(
        jnp.dot(cond_cols, mod_local, preferred_element_type=jnp.float32),
        "batch",
        scatter_dimension=0,
        tiled=True,
    )
    mod_full = lax.all_gather(
        mod_mine.reshape(req_local, mod_count, head_cols), "tensor", axis=2, tiled=True
    )
    positions = jnp.arange(max_len, dtype=jnp.int32)
    live_mask = positions[None, :] < lengths[:, None]
    own_start = tensor_at * rows_local
    hidden_state = (
        jnp.einsum("rpl,pd->rld", latents, embed_weight, precision=lax.Precision.HIGHEST)
        + position_table(max_len, width)[None]
    )
    for layer_at in range(layer_count):
        modulation = mod_full[:, 6 * layer_at : 6 * layer_at + 6]
        normed = modulate(hidden_state, modulation[:, 0], modulation[:, 1]).astype(jnp.bfloat16)
        projected = rows_product(
            normed.reshape(req_local * max_len, width),
            qkv_weight[layer_at].reshape(width_piece, 3 * head_cols),
        ).astype(jnp.bfloat16)
        projected = projected.reshape(req_local, max_len, 3, heads_local, HDIM)
        attended = lax.map(attend, (projected, live_mask))
        branch = cols_product(
            attended.reshape(req_local * max_len, head_cols), proj_weight[layer_at]
        ).reshape(req_local, max_len, width)
        branch = lax.psum(branch.astype(jnp.bfloat16), "tensor").astype(jnp.float32)
        hidden_state = hidden_state + modulation[:, 2][:, None, :] * branch
        normed = modulate(hidden_state, modulation[:, 3], modulation[:, 4]).astype(jnp.bfloat16)
        hidden_units = jax.nn.gelu(
            rows_product(normed.reshape(req_local * max_len, width), up_weight[layer_at]),
            approximate=True,
        ).astype(jnp.bfloat16)
        branch = cols_product(hidden_units, down_weight[layer_at]).reshape(
            req_local, max_len, width
        )
        branch = lax.psum(branch.astype(jnp.bfloat16), "tensor").astype(jnp.float32)
        hidden_state = hidden_state + modulation[:, 5][:, None, :] * branch
    hidden_state = lax.dynamic_slice_in_dim(hidden_state, own_start, rows_local, 1)
    final_in = modulate(
        hidden_state, mod_full[:, 6 * layer_count], mod_full[:, 6 * layer_count + 1]
    ).astype(jnp.bfloat16)
    noise_own = jnp.einsum(
        "rld,dp->rpl", final_in, output_weight, preferred_element_type=jnp.float32
    )
    return finish(latents, lengths, timesteps, guidance, noise_own, rows_local)


def alpha_table():
    beta_values = np.linspace(0.0001, 0.02, TRAIN_STEPS, dtype=np.float32)
    return np.cumprod(np.float32(1.0) - beta_values, dtype=np.float32)


def finish(latents, lengths, timesteps, guidance, noise_own, rows_local):
    patch_size, max_len = latents.shape[1:]
    guide_at = lax.axis_index("guide")
    is_first = guide_at == 0
    own_start = lax.axis_index("tensor") * rows_local
    own_latents = lax.dynamic_slice_in_dim(latents, own_start, rows_local, 2)
    own_live = (own_start + jnp.arange(rows_local, dtype=jnp.int32))[None, :] < lengths[:, None]
    half_patch = patch_size // 2
    mine_noise = lax.dynamic_slice_in_dim(noise_own, guide_at * half_patch, half_patch, 1)
    other_noise = lax.dynamic_slice_in_dim(noise_own, (1 - guide_at) * half_patch, half_patch, 1)
    partner_noise = from_partner(other_noise, "guide", 0)
    cond_noise = jnp.where(is_first, mine_noise, partner_noise)
    uncond_noise = jnp.where(is_first, partner_noise, mine_noise)
    live_out = own_live[:, None, :]
    guided = uncond_noise + guidance[:, None, None] * (cond_noise - uncond_noise)
    guided = jnp.where(live_out, guided, 0.0)
    half_latents = lax.dynamic_slice_in_dim(own_latents, guide_at * half_patch, half_patch, 1)
    alpha_bar = jnp.asarray(alpha_table())
    step_ids = jnp.arange(TRAIN_STEPS, dtype=jnp.int32)
    alpha_now = jnp.sum(
        jnp.where(step_ids[None, :] == timesteps[:, None], alpha_bar[None, :], 0.0), axis=1
    )[:, None, None]
    alpha_prev = jnp.sum(
        jnp.where(step_ids[None, :] == (timesteps - STRIDE)[:, None], alpha_bar[None, :], 0.0),
        axis=1,
    )[:, None, None]
    start_est = (half_latents - jnp.sqrt(1.0 - alpha_now) * guided) / jnp.sqrt(alpha_now)
    previous = jnp.sqrt(alpha_prev) * start_est + jnp.sqrt(1.0 - alpha_prev) * guided
    previous = jnp.where(live_out, previous, 0.0)
    return (guided, previous)


def exchange(block, axis, bit):
    count = lax.axis_size(axis)
    return lax.ppermute(block, axis, [(at, at ^ bit) for at in range(count)])


def after(value, *earlier):
    return lax.optimization_barrier((value, *earlier))[0]


HOLDS = {"own": (0,), "two": (4,), "pair": (0, 4), "four": (2, 6)}

PLAN = (
    ((("own", 0),), (("own", 0),)),
    ((("pair", 0),), (("two", 0), ("own", 1))),
    ((("own", 1),), (("four", 0),)),
    ((("pair", 1), ("own", 2)), (("two", 1), ("own", 2), ("own", 3))),
    ((("pair", 2), ("own", 3)), (("four", 1), ("two", 2))),
    ((("pair", 3), ("own", 4)), (("four", 2), ("two", 3))),
    ((("pair", 4), ("own", 5)), (("four", 3), ("pair", 4))),
    ((("pair", 5),), (("four", 4), ("pair", 5))),
    ((), (("four", 5),)),
)
READY = ((0,), (1, 2), (3,), (), (4, 5))


class Stream:
    def __init__(self, make_own):
        self.make_own, self.at, self.last = make_own, 0, None
        self.values, self.arrived, self.sent = {}, {}, ()
        self.blocks = [[] for _ in make_own]

    def hand_over(self, array, parts, flip, anchor):
        earlier = []
        other = self.last = exchange(after(array, *earlier) if earlier else array, "guide", 1)
        at = 0
        for kind, piece in parts:
            for distance in HOLDS[kind]:
                for which, buffer in enumerate((array, other)):
                    self.blocks[piece].append((buffer, at, distance ^ flip, which))
                at += 1

    def step(self, *first):
        over_z, over_x = PLAN[self.at] if self.at < len(PLAN) else ((), ())
        for piece in READY[self.at] if self.at < len(READY) else ():
            self.values["own", piece] = self.make_own[piece]()
        self.at += 1
        self.values, arrived, _ = lax.optimization_barrier((self.values, self.arrived, first))
        self.values = values = dict(self.values)
        for (kind, piece), value in arrived.items():
            if kind == "own":
                values["two", piece] = value
                values["pair", piece] = jnp.concatenate([values["own", piece], value], axis=0)
            elif kind == "pair":
                values["four", piece] = value
        came = arrived.get("x")
        self.arrived, anchor = {}, None
        source = [values[part] for part in over_x]
        if source:
            source = source[0] if len(source) == 1 else jnp.concatenate(source, axis=0)
            self.arrived["x", ""] = exchange(source, "batch", 1)
        for kind, piece in over_z:
            sent = exchange(values[kind, piece], "batch", 4 if kind == "own" else 2)
            self.arrived[kind, piece] = sent
            anchor = sent if anchor is None else anchor
        if ("x", "") in arrived:
            self.hand_over(arrived["x", ""], self.sent, 1, None)
        if over_x:
            self.hand_over(source, over_x, 0, anchor)
        self.sent = over_x

    def operands(self, piece):
        arrays, places = [], []
        for buffer, at, distance, which in self.blocks[piece]:
            found = [n for n, array in enumerate(arrays) if array is buffer]
            if not found:
                arrays.append(buffer)
            places.append((found[0] if found else len(arrays) - 1, at, distance, which))
        return arrays, places


def fetch(weights, slots, buffers, places, batch_at, arrivals):
    rows = weights.shape[1] // (len(places) // 2)
    copies = []
    for number, (array, at, distance, which) in enumerate(places):
        row = pl.multiple_of((batch_at ^ distance) * rows, 16)
        copies.append(
            pltpu.make_async_copy(
                buffers[array].at[pl.ds(at * rows, rows), :],
                weights.at[slots[which], pl.ds(row, rows), :],
                arrivals.at[number],
            )
        )
        copies[-1].start()
    return copies


def normalized(hidden, shift, scale):
    center = hidden - jnp.mean(hidden, axis=-1, keepdims=True)
    spread = jnp.mean(center * center, axis=-1, keepdims=True)
    return center * lax.rsqrt(spread + norm_epsilon) * (1.0 + scale) + shift


def dot_nt(left, right):
    return lax.dot_general(
        left, right, (((1,), (1,)), ((), ())), preferred_element_type=jnp.float32
    )


def kernel_call(body, outs, scratch, operands, buffers, flops, bytes_moved):
    specs = [pl.BlockSpec(memory_space=pltpu.SMEM)]
    specs += [pl.BlockSpec(memory_space=pltpu.VMEM) for _ in operands[1:]]
    specs += [pl.BlockSpec(memory_space=pl.ANY) for _ in buffers]
    if buffers:
        scratch = scratch + [pltpu.SemaphoreType.DMA((16,))]
    return pl.pallas_call(
        body,
        out_shape=outs,
        in_specs=specs,
        out_specs=jax.tree.map(lambda _: pl.BlockSpec(memory_space=pltpu.VMEM), outs),
        scratch_shapes=scratch,
        cost_estimate=pl.CostEstimate(
            flops=int(flops), bytes_accessed=int(bytes_moved), transcendentals=0
        ),
        compiler_params=pltpu.CompilerParams(vmem_limit_bytes=44 * 2**20),
    )(*operands, *buffers)


def enter(hidden, branches, mods, row, hidden_out, normed):
    state = hidden[...]
    if branches:
        total = branches[0][...].astype(jnp.float32) + branches[1][...].astype(jnp.float32)
        state = state + mods[row - 1 : row, :] * total
        hidden_out[...] = state
    normed[...] = normalized(state, mods[row : row + 1, :], mods[row + 1 : row + 2, :]).astype(
        jnp.bfloat16
    )


def qkv_kernel(places, array_count, layer, heads, branch_count, ids, hidden, mods, *refs):
    branches, refs = refs[:branch_count], refs[branch_count:]
    buffers, refs = refs[:array_count], refs[array_count:]
    hidden_out = None
    if branches:
        hidden_out, refs = refs[0], refs[1:]
    heads_out, proj_out, weights, normed, projected, arrivals = refs
    width = hidden.shape[1]
    half = width // 2
    copies = fetch(weights, [ids[1], 1 - ids[1]], buffers, places, ids[0], arrivals)
    enter(hidden, branches, mods, 6 * layer, hidden_out, normed)
    for copy in copies:
        copy.wait()
    proj_out[...] = weights[1, :, half:]

    def step(at, carry):
        lo = pl.multiple_of(at * 384, 128)
        projected[:, pl.ds(lo, 384)] = jnp.dot(
            normed[...], weights[0, :, pl.ds(lo, 384)], preferred_element_type=jnp.float32
        ).astype(jnp.bfloat16)
        return carry

    lax.fori_loop(0, width // 384, step, 0)
    projected[:, width:] = jnp.dot(
        normed[...], weights[1, :, :half], preferred_element_type=jnp.float32
    ).astype(jnp.bfloat16)
    for at in range(3 * heads):
        heads_out[at] = projected[:, at * HDIM : (at + 1) * HDIM]


def attention_kernel(heads, ids, heads_in, proj, partial, attended):
    keys = heads_in.shape[1]
    factor = math.log2(math.e) / math.sqrt(HDIM)
    live = lax.broadcasted_iota(jnp.int32, (1, keys), 1) < ids[3]
    for at in range(heads):
        scores = dot_nt(heads_in[at], heads_in[heads + at])
        scores = jnp.where(live, scores * factor, -jnp.inf)
        raised = jnp.exp2(scores - jnp.max(scores, axis=-1, keepdims=True))
        total = jnp.sum(raised, axis=-1, keepdims=True)
        out = jnp.dot(
            raised.astype(jnp.bfloat16), heads_in[2 * heads + at], preferred_element_type=jnp.float32
        )
        attended[:, at * HDIM : (at + 1) * HDIM] = (out / total).astype(jnp.bfloat16)
    partial[...] = dot_nt(attended[...], proj[...]).astype(jnp.bfloat16)


def up_kernel(places, array_count, layer, ids, hidden, mods, *refs):
    branches, refs = refs[:2], refs[2:]
    buffers, refs = refs[:array_count], refs[array_count:]
    hidden_out, units, weights, normed, arrivals = refs
    width = hidden.shape[1]
    copies = fetch(weights, [0, 1], buffers, places, ids[0], arrivals)
    enter(hidden, branches, mods, 6 * layer + 3, hidden_out, normed)
    for copy in copies:
        copy.wait()
    for half in range(2):

        def step(at, carry):
            lo = pl.multiple_of(at * 384, 128)
            product = jnp.dot(
                normed[...], weights[half, :, pl.ds(lo, 384)], preferred_element_type=jnp.float32
            )
            inner = math.sqrt(2.0 / math.pi) * (product + 0.044715 * product * product * product)
            units[half, :, pl.ds(lo, 384)] = (0.5 * product * (1.0 + jnp.tanh(inner))).astype(
                jnp.bfloat16
            )
            return carry

        lax.fori_loop(0, width // 384, step, 0)


def down_kernel(places, array_count, ids, units, *refs):
    buffers, (partial, weights, arrivals) = refs[:array_count], refs[array_count:]
    width = partial.shape[1]
    for copy in fetch(weights, [0, 1], buffers, places, ids[0], arrivals):
        copy.wait()

    def step(at, carry):
        lo = pl.multiple_of(at * 384, 128)
        product = dot_nt(units[0], weights[0, pl.ds(lo, 384), :])
        product = product + dot_nt(units[1], weights[1, pl.ds(lo, 384), :])
        partial[:, pl.ds(lo, 384)] = product.astype(jnp.bfloat16)
        return carry

    lax.fori_loop(0, width // 384, step, 0)


def modulation_sums(columns, modulation_weight, final_modulation):
    layer_count, _, _, head_cols = modulation_weight.shape
    blocks = jnp.einsum(
        "rk,lkjc->rljc", columns, modulation_weight, preferred_element_type=jnp.float32
    ).reshape(columns.shape[0], 6 * layer_count, head_cols)
    finals = jnp.einsum("rk,kjc->rjc", columns, final_modulation, preferred_element_type=jnp.float32)
    return jnp.concatenate([blocks, finals], axis=1)


def all_columns(mine):
    other = exchange(mine, "tensor", 1)
    first = lax.axis_index("tensor") == 0
    return jnp.concatenate(
        [jnp.where(first, mine, other), jnp.where(first, other, mine)], axis=1
    )


def fast_local(
    latents,
    lengths,
    timesteps,
    guidance,
    condition,
    embed_weight,
    modulation_weight,
    final_modulation,
    qkv_weight,
    proj_weight,
    up_weight,
    down_weight,
    output_weight,
):
    tensor_at = lax.axis_index("tensor")
    batch_at = lax.axis_index("batch")
    guide_at = lax.axis_index("guide")
    _, patch_size, max_len = latents.shape
    width = embed_weight.shape[1]
    half = width // 2
    layer_count = qkv_weight.shape[0]
    heads = half // HDIM
    rows_own = max_len // 2
    width_piece = qkv_weight.shape[1]
    first = guide_at == 0
    ids = jnp.stack([batch_at, guide_at, tensor_at, lengths[0]]).astype(jnp.int32)
    bf16, f32 = jnp.bfloat16, jnp.float32

    def attention_piece(layer):
        queries_keys = qkv_weight[layer, :, :2].reshape(width_piece, width)
        values_proj = jnp.concatenate([qkv_weight[layer, :, 2], proj_weight[layer].T], axis=1)
        return jnp.where(first, queries_keys, values_proj)

    def up_piece(layer):
        return lax.dynamic_slice_in_dim(up_weight[layer], guide_at * width, width, 1)

    def down_piece(layer):
        return lax.dynamic_slice_in_dim(down_weight[layer], guide_at * width, width, 0).T

    stream = Stream(
        [
            functools.partial(make, layer)
            for layer in range(layer_count)
            for make in (attention_piece, up_piece, down_piece)
        ]
    )
    weight_bytes = 4 * width * width
    shape = jax.ShapeDtypeStruct
    two_weights = pltpu.VMEM((2, width, width), bf16)
    normed = pltpu.VMEM((max_len, width), bf16)

    def attention_block(layer, hidden, mods, branches):
        outs = [shape((3 * heads, max_len, HDIM), bf16), shape((width, half), bf16)]
        if branches:
            outs = [shape((max_len, width), f32)] + outs
        arrays, places = stream.operands(3 * layer)
        results = kernel_call(
            functools.partial(qkv_kernel, places, len(arrays), layer, heads, len(branches)),
            outs,
            [two_weights, normed, pltpu.VMEM((max_len, 3 * half), bf16)],
            [ids, hidden, mods, *branches],
            arrays,
            2 * max_len * width * 3 * half,
            weight_bytes,
        )
        partial = kernel_call(
            functools.partial(attention_kernel, heads),
            shape((max_len, width), bf16),
            [pltpu.VMEM((max_len, half), bf16)],
            [ids, *results[-2:]],
            [],
            4 * max_len * max_len * half + 2 * max_len * half * width,
            weight_bytes,
        )
        return results[0] if branches else hidden, partial

    def both(partial):
        return [partial, exchange(partial, "tensor", 1)]

    def up_block(layer, hidden, mods, branches):
        arrays, places = stream.operands(3 * layer + 1)
        return kernel_call(
            functools.partial(up_kernel, places, len(arrays), layer),
            [shape((max_len, width), f32), shape((2, max_len, width), bf16)],
            [two_weights, normed],
            [ids, hidden, mods, *branches],
            arrays,
            4 * max_len * width * width,
            weight_bytes,
        )

    def down_block(layer, units):
        arrays, places = stream.operands(3 * layer + 2)
        return kernel_call(
            functools.partial(down_kernel, places, len(arrays)),
            shape((max_len, width), bf16),
            [two_weights],
            [ids, units],
            arrays,
            4 * max_len * width * width,
            weight_bytes,
        )

    activated = jax.nn.silu(condition[0]).astype(bf16).reshape(-1, width_piece)
    stream.step()
    columns = lax.all_to_all(activated, "batch", 0, 0, tiled=True)
    stream.step(columns)
    sums = modulation_sums(columns, modulation_weight, final_modulation)
    mine = jnp.sum(lax.all_to_all(sums, "batch", 0, 0, tiled=True), axis=0)
    stream.step()
    hidden = jnp.einsum(
        "pl,pd->ld", latents[0], embed_weight, precision=lax.Precision.HIGHEST
    ) + position_table(max_len, width)
    stream.step(mine, hidden)
    mods = all_columns(mine)
    hidden, partial = attention_block(0, hidden, mods, [])
    stream.step(partial)
    branches = both(partial)
    stream.step(branches)
    hidden, units = up_block(0, hidden, mods, branches)
    stream.step(units)
    partial = down_block(0, units)
    stream.step(partial)
    hidden, partial = attention_block(1, hidden, mods, both(partial))
    stream.step(partial)
    branches = both(partial)
    stream.step()
    hidden, units = up_block(1, hidden, mods, branches)
    partial = down_block(1, units)
    own_start = tensor_at * rows_own
    mine = lax.dynamic_slice_in_dim(partial, own_start, rows_own, 0)
    theirs = exchange(
        lax.dynamic_slice_in_dim(partial, (1 - tensor_at) * rows_own, rows_own, 0), "tensor", 1
    )
    hidden = lax.dynamic_slice_in_dim(hidden, own_start, rows_own, 0)
    hidden = hidden + mods[6 * layer_count - 1][None, :] * (
        mine.astype(f32) + theirs.astype(f32)
    )
    final_in = normalized(
        hidden, mods[6 * layer_count][None, :], mods[6 * layer_count + 1][None, :]
    ).astype(bf16)
    noise_own = lax.dot_general(
        output_weight, final_in, (((0,), (1,)), ((), ())), preferred_element_type=f32
    )[None]
    return finish(latents, lengths, timesteps, guidance, noise_own, rows_own)


def solution(mesh):
    in_specs = (
        P("batch", None, None),
        P("batch"),
        P("batch"),
        P("batch"),
        P("guide", "batch", None),
        P(),
        P(None, "batch", None, "tensor"),
        P("batch", None, "tensor"),
        P(None, "batch", None, "tensor"),
        P(None, "tensor", "batch"),
        P(None, "batch", "tensor"),
        P(None, "tensor", "batch"),
        P(),
    )
    out_specs = (P("batch", "guide", "tensor"), P("batch", "guide", "tensor"))
    sizes = mesh.shape
    small = sizes["batch"] == 8 and sizes["tensor"] == 2
    body = fast_local if small else local
    return jax.shard_map(body, mesh=mesh, in_specs=in_specs, out_specs=out_specs, check_vma=False)
```

```python
import functools
import math

import jax
import jax.numpy as jnp
import numpy as np
from jax import lax
from jax.experimental import pallas as pl
from jax.experimental.pallas import tpu as pltpu
from jax.sharding import PartitionSpec as P

HDIM = 72
TRAIN_STEPS = 1000
STRIDE = 20


norm_epsilon = 1e-06


def from_partner(block, axis, distance):
    count = lax.axis_size(axis)
    route = []
    for low in range(count):
        high = low | 1 << distance
        if high != low and high < count:
            route += [(low, high), (high, low)]
    return lax.ppermute(block, axis, route)


def layer_norm(values):
    center = values - jnp.mean(values, axis=-1, keepdims=True)
    spread = jnp.mean(center * center, axis=-1, keepdims=True)
    return center * lax.rsqrt(spread + norm_epsilon)


def modulate(values, shift, scale):
    return layer_norm(values) * (1.0 + scale[:, None, :]) + shift[:, None, :]


def position_values(row_count, width):
    half_width = width // 2
    frequency = np.exp(
        np.arange(half_width, dtype=np.float32) * np.float32(-math.log(10000.0) / half_width)
    )
    angles = np.arange(row_count, dtype=np.float32)[:, None] * frequency[None, :]
    return np.concatenate([np.sin(angles), np.cos(angles)], axis=1).astype(np.float32)


def position_table(row_count, width):
    rows_at = jnp.arange(row_count, dtype=jnp.int32).astype(jnp.float32)
    half_width = width // 2
    frequency = jnp.exp(
        jnp.arange(half_width, dtype=jnp.float32) * (-math.log(10000.0) / half_width)
    )
    angles = rows_at[:, None] * frequency[None, :]
    return jnp.concatenate([jnp.sin(angles), jnp.cos(angles)], axis=1)


def attend(operands):
    projected_item, key_live = operands
    score_scale = 1.0 / math.sqrt(HDIM)
    scores = (
        jnp.einsum(
            "qhd,khd->hqk",
            projected_item[:, 0],
            projected_item[:, 1],
            preferred_element_type=jnp.float32,
        )
        * score_scale
    )
    scores = jnp.where(key_live[None, None, :], scores, -jnp.inf)
    row_max = jnp.max(scores, axis=-1, keepdims=True)
    exp_scores = jnp.exp(scores - row_max)
    probabilities = (exp_scores / jnp.sum(exp_scores, axis=-1, keepdims=True)).astype(jnp.bfloat16)
    attended = jnp.einsum(
        "hqk,khd->qhd", probabilities, projected_item[:, 2], preferred_element_type=jnp.float32
    )
    return attended.astype(jnp.bfloat16).reshape(
        attended.shape[0], attended.shape[1] * attended.shape[2]
    )


def local(
    latents,
    lengths,
    timesteps,
    guidance,
    condition,
    embed_weight,
    modulation_weight,
    final_modulation,
    qkv_weight,
    proj_weight,
    up_weight,
    down_weight,
    output_weight,
):
    tensor_count = lax.axis_size("tensor")
    batch_count = lax.axis_size("batch")
    tensor_at = lax.axis_index("tensor")
    batch_at = lax.axis_index("batch")
    req_local, patch_size, max_len = latents.shape
    width = embed_weight.shape[1]
    layer_count = qkv_weight.shape[0]
    head_cols = qkv_weight.shape[3]
    heads_local = head_cols // HDIM
    rows_local = max_len // tensor_count
    width_piece = width // batch_count
    mod_count = 6 * layer_count + 2

    def rows_product(activation, shard):
        return jnp.dot(
            activation,
            lax.all_gather(shard, "batch", axis=0, tiled=True),
            preferred_element_type=jnp.float32,
        )

    def cols_product(activation, shard):
        return jnp.dot(
            activation,
            lax.all_gather(shard, "batch", axis=1, tiled=True),
            preferred_element_type=jnp.float32,
        )

    cond_act = jax.nn.silu(condition[0]).astype(jnp.bfloat16)
    cond_all = lax.all_gather(cond_act, "batch", axis=0, tiled=True)
    cond_cols = lax.dynamic_slice_in_dim(cond_all, batch_at * width_piece, width_piece, 1)
    block_local = jnp.transpose(modulation_weight, (1, 0, 2, 3)).reshape(
        width_piece, 6 * layer_count * head_cols
    )
    mod_local = jnp.concatenate(
        [block_local, final_modulation.reshape(width_piece, 2 * head_cols)], axis=1
    )
    mod_mine = lax.psum_scatter(
        jnp.dot(cond_cols, mod_local, preferred_element_type=jnp.float32),
        "batch",
        scatter_dimension=0,
        tiled=True,
    )
    mod_full = lax.all_gather(
        mod_mine.reshape(req_local, mod_count, head_cols), "tensor", axis=2, tiled=True
    )
    positions = jnp.arange(max_len, dtype=jnp.int32)
    live_mask = positions[None, :] < lengths[:, None]
    own_start = tensor_at * rows_local
    hidden_state = (
        jnp.einsum("rpl,pd->rld", latents, embed_weight, precision=lax.Precision.HIGHEST)
        + position_table(max_len, width)[None]
    )
    for layer_at in range(layer_count):
        modulation = mod_full[:, 6 * layer_at : 6 * layer_at + 6]
        normed = modulate(hidden_state, modulation[:, 0], modulation[:, 1]).astype(jnp.bfloat16)
        projected = rows_product(
            normed.reshape(req_local * max_len, width),
            qkv_weight[layer_at].reshape(width_piece, 3 * head_cols),
        ).astype(jnp.bfloat16)
        projected = projected.reshape(req_local, max_len, 3, heads_local, HDIM)
        attended = lax.map(attend, (projected, live_mask))
        branch = cols_product(
            attended.reshape(req_local * max_len, head_cols), proj_weight[layer_at]
        ).reshape(req_local, max_len, width)
        branch = lax.psum(branch.astype(jnp.bfloat16), "tensor").astype(jnp.float32)
        hidden_state = hidden_state + modulation[:, 2][:, None, :] * branch
        normed = modulate(hidden_state, modulation[:, 3], modulation[:, 4]).astype(jnp.bfloat16)
        hidden_units = jax.nn.gelu(
            rows_product(normed.reshape(req_local * max_len, width), up_weight[layer_at]),
            approximate=True,
        ).astype(jnp.bfloat16)
        branch = cols_product(hidden_units, down_weight[layer_at]).reshape(
            req_local, max_len, width
        )
        branch = lax.psum(branch.astype(jnp.bfloat16), "tensor").astype(jnp.float32)
        hidden_state = hidden_state + modulation[:, 5][:, None, :] * branch
    hidden_state = lax.dynamic_slice_in_dim(hidden_state, own_start, rows_local, 1)
    final_in = modulate(
        hidden_state, mod_full[:, 6 * layer_count], mod_full[:, 6 * layer_count + 1]
    ).astype(jnp.bfloat16)
    noise_own = jnp.einsum(
        "rld,dp->rpl", final_in, output_weight, preferred_element_type=jnp.float32
    )
    return finish(latents, lengths, timesteps, guidance, noise_own, rows_local)


def alpha_table():
    beta_values = np.linspace(0.0001, 0.02, TRAIN_STEPS, dtype=np.float32)
    return np.cumprod(np.float32(1.0) - beta_values, dtype=np.float32)


def finish(latents, lengths, timesteps, guidance, noise_own, rows_local):
    patch_size, max_len = latents.shape[1:]
    guide_at = lax.axis_index("guide")
    is_first = guide_at == 0
    own_start = lax.axis_index("tensor") * rows_local
    own_latents = lax.dynamic_slice_in_dim(latents, own_start, rows_local, 2)
    own_live = (own_start + jnp.arange(rows_local, dtype=jnp.int32))[None, :] < lengths[:, None]
    half_patch = patch_size // 2
    mine_noise = lax.dynamic_slice_in_dim(noise_own, guide_at * half_patch, half_patch, 1)
    other_noise = lax.dynamic_slice_in_dim(noise_own, (1 - guide_at) * half_patch, half_patch, 1)
    partner_noise = from_partner(other_noise, "guide", 0)
    cond_noise = jnp.where(is_first, mine_noise, partner_noise)
    uncond_noise = jnp.where(is_first, partner_noise, mine_noise)
    live_out = own_live[:, None, :]
    guided = uncond_noise + guidance[:, None, None] * (cond_noise - uncond_noise)
    guided = jnp.where(live_out, guided, 0.0)
    half_latents = lax.dynamic_slice_in_dim(own_latents, guide_at * half_patch, half_patch, 1)
    alpha_bar = jnp.asarray(alpha_table())
    step_ids = jnp.arange(TRAIN_STEPS, dtype=jnp.int32)
    alpha_now = jnp.sum(
        jnp.where(step_ids[None, :] == timesteps[:, None], alpha_bar[None, :], 0.0), axis=1
    )[:, None, None]
    alpha_prev = jnp.sum(
        jnp.where(step_ids[None, :] == (timesteps - STRIDE)[:, None], alpha_bar[None, :], 0.0),
        axis=1,
    )[:, None, None]
    start_est = (half_latents - jnp.sqrt(1.0 - alpha_now) * guided) / jnp.sqrt(alpha_now)
    previous = jnp.sqrt(alpha_prev) * start_est + jnp.sqrt(1.0 - alpha_prev) * guided
    previous = jnp.where(live_out, previous, 0.0)
    return (guided, previous)


def exchange(block, axis, bit):
    count = lax.axis_size(axis)
    return lax.ppermute(block, axis, [(at, at ^ bit) for at in range(count)])


HOLDS = {"own": (0,), "two": (4,), "pair": (0, 4), "four": (2, 6)}

PLAN = (
    ((("own", 0),), (("own", 0),)),
    ((("pair", 0),), (("two", 0), ("own", 1))),
    ((("own", 1),), (("four", 0),)),
    ((("pair", 1), ("own", 2)), (("two", 1), ("own", 2), ("own", 3))),
    ((("pair", 2), ("own", 3)), (("four", 1), ("two", 2))),
    ((("pair", 3), ("own", 4)), (("four", 2), ("two", 3))),
    ((("pair", 4), ("own", 5)), (("four", 3), ("pair", 4), ("own", 5))),
    ((("pair", 5),), (("four", 4), ("two", 5))),
    ((), (("four", 5),)),
)
READY = ((0,), (1, 2), (3,), (), (4, 5))


class Stream:
    def __init__(self, make_own):
        self.make_own, self.at = make_own, 0
        self.values, self.arrived, self.sent = {}, {}, ()
        self.blocks = [[] for _ in make_own]

    def hand_over(self, array, parts, flip):
        other = exchange(array, "guide", 1)
        at = 0
        for kind, piece in parts:
            for distance in HOLDS[kind]:
                for which, buffer in enumerate((array, other)):
                    self.blocks[piece].append((buffer, at, distance ^ flip, which))
                at += 1

    def step(self, *first):
        over_z, over_x = PLAN[self.at] if self.at < len(PLAN) else ((), ())
        for piece in READY[self.at] if self.at < len(READY) else ():
            self.values["own", piece] = self.make_own[piece]()
        self.at += 1
        self.values, arrived, _ = lax.optimization_barrier((self.values, self.arrived, first))
        self.values = values = dict(self.values)
        for (kind, piece), value in arrived.items():
            if kind == "own":
                values["two", piece] = value
                values["pair", piece] = jnp.concatenate([values["own", piece], value], axis=0)
            elif kind == "pair":
                values["four", piece] = value
        self.arrived = {}
        source = [values[part] for part in over_x]
        if source:
            source = source[0] if len(source) == 1 else jnp.concatenate(source, axis=0)
            self.arrived["x", ""] = exchange(source, "batch", 1)
        for kind, piece in over_z:
            bit = 4 if kind == "own" else 2
            self.arrived[kind, piece] = exchange(values[kind, piece], "batch", bit)
        if ("x", "") in arrived:
            self.hand_over(arrived["x", ""], self.sent, 1)
        if over_x:
            self.hand_over(source, over_x, 0)
        self.sent = over_x

    def operands(self, piece):
        arrays, places = [], []
        for buffer, at, distance, which in self.blocks[piece]:
            found = [n for n, array in enumerate(arrays) if array is buffer]
            if not found:
                arrays.append(buffer)
            places.append((found[0] if found else len(arrays) - 1, at, distance, which))
        return arrays, places


def fetch(weights, slots, buffers, places, batch_at, arrivals):
    rows = weights.shape[1] // (len(places) // 2)
    copies = []
    for number, (array, at, distance, which) in enumerate(places):
        row = pl.multiple_of((batch_at ^ distance) * rows, 16)
        copies.append(
            pltpu.make_async_copy(
                buffers[array].at[pl.ds(at * rows, rows), :],
                weights.at[slots[which], pl.ds(row, rows), :],
                arrivals.at[number],
            )
        )
        copies[-1].start()
    return copies


def normalized(hidden, shift, scale):
    center = hidden - jnp.mean(hidden, axis=-1, keepdims=True)
    spread = jnp.mean(center * center, axis=-1, keepdims=True)
    return center * lax.rsqrt(spread + norm_epsilon) * (1.0 + scale) + shift


def dot_nt(left, right):
    return lax.dot_general(
        left, right, (((1,), (1,)), ((), ())), preferred_element_type=jnp.float32
    )


def kernel_call(body, outs, scratch, operands, buffers, fetches, flops, bytes_moved):
    specs = [pl.BlockSpec(memory_space=pltpu.SMEM)]
    specs += [pl.BlockSpec(memory_space=pltpu.VMEM) for _ in operands[1:]]
    specs += [pl.BlockSpec(memory_space=pl.ANY) for _ in buffers]
    scratch = scratch + [pltpu.SemaphoreType.DMA((16,))] * fetches
    return pl.pallas_call(
        body,
        out_shape=outs,
        in_specs=specs,
        out_specs=jax.tree.map(lambda _: pl.BlockSpec(memory_space=pltpu.VMEM), outs),
        scratch_shapes=scratch,
        cost_estimate=pl.CostEstimate(
            flops=int(flops), bytes_accessed=int(bytes_moved), transcendentals=0
        ),
        compiler_params=pltpu.CompilerParams(vmem_limit_bytes=44 * 2**20),
    )(*operands, *buffers)


def enter(hidden, branches, mods, row, hidden_out, normed):
    state = hidden[...]
    if branches:
        total = branches[0][...].astype(jnp.float32) + branches[1][...].astype(jnp.float32)
        state = state + mods[row - 1 : row, :] * total
        hidden_out[...] = state
    normed[...] = normalized(state, mods[row : row + 1, :], mods[row + 1 : row + 2, :]).astype(
        jnp.bfloat16
    )


def attention_kernel(places, array_count, layer, heads, branch_count, ids, hidden, mods, *refs):
    branches, refs = refs[:branch_count], refs[branch_count:]
    buffers, refs = refs[:array_count], refs[array_count:]
    hidden_out = None
    if branches:
        hidden_out, refs = refs[0], refs[1:]
    partial, weights, normed, projected, split, attended, arrivals = refs
    width, keys = hidden.shape[1], hidden.shape[0]
    half = width // 2
    copies = fetch(weights, [ids[1], 1 - ids[1]], buffers, places, ids[0], arrivals)
    enter(hidden, branches, mods, 6 * layer, hidden_out, normed)
    for copy in copies:
        copy.wait()

    def step(at, carry):
        lo = pl.multiple_of(at * 384, 128)
        projected[:, pl.ds(lo, 384)] = jnp.dot(
            normed[...], weights[0, :, pl.ds(lo, 384)], preferred_element_type=jnp.float32
        ).astype(jnp.bfloat16)
        return carry

    lax.fori_loop(0, width // 384, step, 0)
    projected[:, width:] = jnp.dot(
        normed[...], weights[1, :, :half], preferred_element_type=jnp.float32
    ).astype(jnp.bfloat16)
    for at in range(3 * heads):
        split[at] = projected[:, at * HDIM : (at + 1) * HDIM]
    factor = math.log2(math.e) / math.sqrt(HDIM)
    live = lax.broadcasted_iota(jnp.int32, (1, keys), 1) < ids[3]
    for at in range(heads):
        scores = dot_nt(split[at], split[heads + at])
        scores = jnp.where(live, scores * factor, -jnp.inf)
        raised = jnp.exp2(scores - jnp.max(scores, axis=-1, keepdims=True))
        total = jnp.sum(raised, axis=-1, keepdims=True)
        out = jnp.dot(
            raised.astype(jnp.bfloat16), split[2 * heads + at], preferred_element_type=jnp.float32
        )
        attended[:, at * HDIM : (at + 1) * HDIM] = (out / total).astype(jnp.bfloat16)
    partial[...] = dot_nt(attended[...], weights[1, :, half:]).astype(jnp.bfloat16)


def expand(normed, weights, units):
    width = normed.shape[1]
    for half in range(2):

        def step(at, carry):
            lo = pl.multiple_of(at * 384, 128)
            product = jnp.dot(
                normed[...], weights[half, :, pl.ds(lo, 384)], preferred_element_type=jnp.float32
            )
            inner = math.sqrt(2.0 / math.pi) * (product + 0.044715 * product * product * product)
            units[half, :, pl.ds(lo, 384)] = (0.5 * product * (1.0 + jnp.tanh(inner))).astype(
                jnp.bfloat16
            )
            return carry

        lax.fori_loop(0, width // 384, step, 0)


def contract(units, weights, partial):
    width = partial.shape[1]

    def step(at, carry):
        lo = pl.multiple_of(at * 384, 128)
        product = dot_nt(units[0], weights[0, pl.ds(lo, 384), :])
        product = product + dot_nt(units[1], weights[1, pl.ds(lo, 384), :])
        partial[:, pl.ds(lo, 384)] = product.astype(jnp.bfloat16)
        return carry

    lax.fori_loop(0, width // 384, step, 0)


def up_kernel(places, array_count, layer, ids, hidden, mods, *refs):
    branches, refs = refs[:2], refs[2:]
    buffers, refs = refs[:array_count], refs[array_count:]
    hidden_out, units, weights, normed, arrivals = refs
    copies = fetch(weights, [0, 1], buffers, places, ids[0], arrivals)
    enter(hidden, branches, mods, 6 * layer + 3, hidden_out, normed)
    for copy in copies:
        copy.wait()
    expand(normed, weights, units)


def down_kernel(places, array_count, ids, units, *refs):
    buffers, (partial, weights, arrivals) = refs[:array_count], refs[array_count:]
    for copy in fetch(weights, [0, 1], buffers, places, ids[0], arrivals):
        copy.wait()
    contract(units, weights, partial)


def mlp_kernel(places, counts, layer, ids, hidden, mods, *refs):
    branches, refs = refs[:2], refs[2:]
    ups, downs, refs = refs[: counts[0]], refs[counts[0] : sum(counts)], refs[sum(counts) :]
    hidden_out, partial, up_weights, down_weights, units, normed, arrivals, more_arrivals = refs
    up_copies = fetch(up_weights, [0, 1], ups, places[0], ids[0], arrivals)
    down_copies = fetch(down_weights, [0, 1], downs, places[1], ids[0], more_arrivals)
    enter(hidden, branches, mods, 6 * layer + 3, hidden_out, normed)
    for copy in up_copies:
        copy.wait()
    expand(normed, up_weights, units)
    for copy in down_copies:
        copy.wait()
    contract(units, down_weights, partial)


def modulation_sums(columns, modulation_weight, final_modulation):
    layer_count, _, _, head_cols = modulation_weight.shape
    blocks = jnp.einsum(
        "rk,lkjc->rljc", columns, modulation_weight, preferred_element_type=jnp.float32
    ).reshape(columns.shape[0], 6 * layer_count, head_cols)
    finals = jnp.einsum("rk,kjc->rjc", columns, final_modulation, preferred_element_type=jnp.float32)
    return jnp.concatenate([blocks, finals], axis=1)


def all_columns(mine):
    other = exchange(mine, "tensor", 1)
    first = lax.axis_index("tensor") == 0
    return jnp.concatenate(
        [jnp.where(first, mine, other), jnp.where(first, other, mine)], axis=1
    )


def fast_local(
    latents,
    lengths,
    timesteps,
    guidance,
    condition,
    embed_weight,
    modulation_weight,
    final_modulation,
    qkv_weight,
    proj_weight,
    up_weight,
    down_weight,
    output_weight,
):
    tensor_at = lax.axis_index("tensor")
    batch_at = lax.axis_index("batch")
    guide_at = lax.axis_index("guide")
    _, patch_size, max_len = latents.shape
    width = embed_weight.shape[1]
    half = width // 2
    layer_count = qkv_weight.shape[0]
    heads = half // HDIM
    rows_own = max_len // 2
    width_piece = qkv_weight.shape[1]
    first = guide_at == 0
    ids = jnp.stack([batch_at, guide_at, tensor_at, lengths[0]]).astype(jnp.int32)
    bf16, f32 = jnp.bfloat16, jnp.float32

    def attention_piece(layer):
        queries_keys = qkv_weight[layer, :, :2].reshape(width_piece, width)
        values_proj = jnp.concatenate([qkv_weight[layer, :, 2], proj_weight[layer].T], axis=1)
        return jnp.where(first, queries_keys, values_proj)

    def up_piece(layer):
        return lax.dynamic_slice_in_dim(up_weight[layer], guide_at * width, width, 1)

    def down_piece(layer):
        return lax.dynamic_slice_in_dim(down_weight[layer], guide_at * width, width, 0).T

    stream = Stream(
        [
            functools.partial(make, layer)
            for layer in range(layer_count)
            for make in (attention_piece, up_piece, down_piece)
        ]
    )
    weight_bytes = 4 * width * width
    shape = jax.ShapeDtypeStruct
    two_weights = pltpu.VMEM((2, width, width), bf16)
    normed = pltpu.VMEM((max_len, width), bf16)

    def attention_block(layer, hidden, mods, branches):
        outs = [shape((max_len, width), bf16)]
        if branches:
            outs = [shape((max_len, width), f32)] + outs
        arrays, places = stream.operands(3 * layer)
        results = kernel_call(
            functools.partial(attention_kernel, places, len(arrays), layer, heads, len(branches)),
            outs,
            [
                two_weights,
                normed,
                pltpu.VMEM((max_len, 3 * half), bf16),
                pltpu.VMEM((3 * heads, max_len, HDIM), bf16),
                pltpu.VMEM((max_len, half), bf16),
            ],
            [ids, hidden, mods, *branches],
            arrays,
            1,
            2 * max_len * width * 4 * half + 4 * max_len * max_len * half,
            weight_bytes,
        )
        return results[0] if branches else hidden, results[-1]

    def both(partial):
        return [partial, exchange(partial, "tensor", 1)]

    def up_block(layer, hidden, mods, branches):
        arrays, places = stream.operands(3 * layer + 1)
        return kernel_call(
            functools.partial(up_kernel, places, len(arrays), layer),
            [shape((max_len, width), f32), shape((2, max_len, width), bf16)],
            [two_weights, normed],
            [ids, hidden, mods, *branches],
            arrays,
            1,
            4 * max_len * width * width,
            weight_bytes,
        )

    def down_block(layer, units):
        arrays, places = stream.operands(3 * layer + 2)
        return kernel_call(
            functools.partial(down_kernel, places, len(arrays)),
            shape((max_len, width), bf16),
            [two_weights],
            [ids, units],
            arrays,
            1,
            4 * max_len * width * width,
            weight_bytes,
        )

    def mlp_block(layer, hidden, mods, branches):
        arrays, places = stream.operands(3 * layer + 1)
        more_arrays, more_places = stream.operands(3 * layer + 2)
        return kernel_call(
            functools.partial(
                mlp_kernel, (places, more_places), (len(arrays), len(more_arrays)), layer
            ),
            [shape((max_len, width), f32), shape((max_len, width), bf16)],
            [two_weights, two_weights, pltpu.VMEM((2, max_len, width), bf16), normed],
            [ids, hidden, mods, *branches],
            arrays + more_arrays,
            2,
            8 * max_len * width * width,
            2 * weight_bytes,
        )

    activated = jax.nn.silu(condition[0]).astype(bf16).reshape(-1, width_piece)
    stream.step()
    columns = lax.all_to_all(activated, "batch", 0, 0, tiled=True)
    stream.step(columns)
    sums = modulation_sums(columns, modulation_weight, final_modulation)
    mine = jnp.sum(lax.all_to_all(sums, "batch", 0, 0, tiled=True), axis=0)
    hidden = jnp.einsum(
        "pl,pd->ld", latents[0], embed_weight, precision=lax.Precision.HIGHEST
    ) + jnp.asarray(position_values(max_len, width))
    stream.step(mine, hidden)
    mods = all_columns(mine)
    stream.step(mods)
    hidden, partial = attention_block(0, hidden, mods, [])
    stream.step(partial)
    branches = both(partial)
    stream.step(branches)
    hidden, units = up_block(0, hidden, mods, branches)
    stream.step(units)
    branches = both(down_block(0, units))
    stream.step(branches)
    hidden, partial = attention_block(1, hidden, mods, branches)
    stream.step(partial)
    branches = both(partial)
    stream.step()
    hidden, partial = mlp_block(1, hidden, mods, branches)
    own_start = tensor_at * rows_own
    mine = lax.dynamic_slice_in_dim(partial, own_start, rows_own, 0)
    theirs = exchange(
        lax.dynamic_slice_in_dim(partial, (1 - tensor_at) * rows_own, rows_own, 0), "tensor", 1
    )
    hidden = lax.dynamic_slice_in_dim(hidden, own_start, rows_own, 0)
    hidden = hidden + mods[6 * layer_count - 1][None, :] * (
        mine.astype(f32) + theirs.astype(f32)
    )
    final_in = normalized(
        hidden, mods[6 * layer_count][None, :], mods[6 * layer_count + 1][None, :]
    ).astype(bf16)
    noise_own = lax.dot_general(
        output_weight, final_in, (((0,), (1,)), ((), ())), preferred_element_type=f32
    )[None]
    return finish(latents, lengths, timesteps, guidance, noise_own, rows_own)


def solution(mesh):
    in_specs = (
        P("batch", None, None),
        P("batch"),
        P("batch"),
        P("batch"),
        P("guide", "batch", None),
        P(),
        P(None, "batch", None, "tensor"),
        P("batch", None, "tensor"),
        P(None, "batch", None, "tensor"),
        P(None, "tensor", "batch"),
        P(None, "batch", "tensor"),
        P(None, "tensor", "batch"),
        P(),
    )
    out_specs = (P("batch", "guide", "tensor"), P("batch", "guide", "tensor"))
    sizes = mesh.shape
    small = sizes["batch"] == 8 and sizes["tensor"] == 2
    body = fast_local if small else local
    return jax.shard_map(body, mesh=mesh, in_specs=in_specs, out_specs=out_specs, check_vma=False)
```

```python
import functools
import math

import jax
import jax.numpy as jnp
import numpy as np
from jax import lax
from jax.experimental import pallas as pl
from jax.experimental.pallas import tpu as pltpu
from jax.sharding import PartitionSpec as P

HDIM = 72
TRAIN_STEPS = 1000
STRIDE = 20


norm_epsilon = 1e-06


def from_partner(block, axis, distance):
    count = lax.axis_size(axis)
    route = []
    for low in range(count):
        high = low | 1 << distance
        if high != low and high < count:
            route += [(low, high), (high, low)]
    return lax.ppermute(block, axis, route)


def layer_norm(values):
    center = values - jnp.mean(values, axis=-1, keepdims=True)
    spread = jnp.mean(center * center, axis=-1, keepdims=True)
    return center * lax.rsqrt(spread + norm_epsilon)


def modulate(values, shift, scale):
    return layer_norm(values) * (1.0 + scale[:, None, :]) + shift[:, None, :]


def position_values(row_count, width):
    half_width = width // 2
    frequency = np.exp(
        np.arange(half_width, dtype=np.float32) * np.float32(-math.log(10000.0) / half_width)
    )
    angles = np.arange(row_count, dtype=np.float32)[:, None] * frequency[None, :]
    return np.concatenate([np.sin(angles), np.cos(angles)], axis=1).astype(np.float32)


def position_table(row_count, width):
    rows_at = jnp.arange(row_count, dtype=jnp.int32).astype(jnp.float32)
    half_width = width // 2
    frequency = jnp.exp(
        jnp.arange(half_width, dtype=jnp.float32) * (-math.log(10000.0) / half_width)
    )
    angles = rows_at[:, None] * frequency[None, :]
    return jnp.concatenate([jnp.sin(angles), jnp.cos(angles)], axis=1)


def attend(operands):
    projected_item, key_live = operands
    score_scale = 1.0 / math.sqrt(HDIM)
    scores = (
        jnp.einsum(
            "qhd,khd->hqk",
            projected_item[:, 0],
            projected_item[:, 1],
            preferred_element_type=jnp.float32,
        )
        * score_scale
    )
    scores = jnp.where(key_live[None, None, :], scores, -jnp.inf)
    row_max = jnp.max(scores, axis=-1, keepdims=True)
    exp_scores = jnp.exp(scores - row_max)
    probabilities = (exp_scores / jnp.sum(exp_scores, axis=-1, keepdims=True)).astype(jnp.bfloat16)
    attended = jnp.einsum(
        "hqk,khd->qhd", probabilities, projected_item[:, 2], preferred_element_type=jnp.float32
    )
    return attended.astype(jnp.bfloat16).reshape(
        attended.shape[0], attended.shape[1] * attended.shape[2]
    )


def local(
    latents,
    lengths,
    timesteps,
    guidance,
    condition,
    embed_weight,
    modulation_weight,
    final_modulation,
    qkv_weight,
    proj_weight,
    up_weight,
    down_weight,
    output_weight,
):
    tensor_count = lax.axis_size("tensor")
    batch_count = lax.axis_size("batch")
    tensor_at = lax.axis_index("tensor")
    batch_at = lax.axis_index("batch")
    req_local, patch_size, max_len = latents.shape
    width = embed_weight.shape[1]
    layer_count = qkv_weight.shape[0]
    head_cols = qkv_weight.shape[3]
    heads_local = head_cols // HDIM
    rows_local = max_len // tensor_count
    width_piece = width // batch_count
    mod_count = 6 * layer_count + 2

    def rows_product(activation, shard):
        return jnp.dot(
            activation,
            lax.all_gather(shard, "batch", axis=0, tiled=True),
            preferred_element_type=jnp.float32,
        )

    def cols_product(activation, shard):
        return jnp.dot(
            activation,
            lax.all_gather(shard, "batch", axis=1, tiled=True),
            preferred_element_type=jnp.float32,
        )

    cond_act = jax.nn.silu(condition[0]).astype(jnp.bfloat16)
    cond_all = lax.all_gather(cond_act, "batch", axis=0, tiled=True)
    cond_cols = lax.dynamic_slice_in_dim(cond_all, batch_at * width_piece, width_piece, 1)
    block_local = jnp.transpose(modulation_weight, (1, 0, 2, 3)).reshape(
        width_piece, 6 * layer_count * head_cols
    )
    mod_local = jnp.concatenate(
        [block_local, final_modulation.reshape(width_piece, 2 * head_cols)], axis=1
    )
    mod_mine = lax.psum_scatter(
        jnp.dot(cond_cols, mod_local, preferred_element_type=jnp.float32),
        "batch",
        scatter_dimension=0,
        tiled=True,
    )
    mod_full = lax.all_gather(
        mod_mine.reshape(req_local, mod_count, head_cols), "tensor", axis=2, tiled=True
    )
    positions = jnp.arange(max_len, dtype=jnp.int32)
    live_mask = positions[None, :] < lengths[:, None]
    own_start = tensor_at * rows_local
    hidden_state = (
        jnp.einsum("rpl,pd->rld", latents, embed_weight, precision=lax.Precision.HIGHEST)
        + position_table(max_len, width)[None]
    )
    for layer_at in range(layer_count):
        modulation = mod_full[:, 6 * layer_at : 6 * layer_at + 6]
        normed = modulate(hidden_state, modulation[:, 0], modulation[:, 1]).astype(jnp.bfloat16)
        projected = rows_product(
            normed.reshape(req_local * max_len, width),
            qkv_weight[layer_at].reshape(width_piece, 3 * head_cols),
        ).astype(jnp.bfloat16)
        projected = projected.reshape(req_local, max_len, 3, heads_local, HDIM)
        attended = lax.map(attend, (projected, live_mask))
        branch = cols_product(
            attended.reshape(req_local * max_len, head_cols), proj_weight[layer_at]
        ).reshape(req_local, max_len, width)
        branch = lax.psum(branch.astype(jnp.bfloat16), "tensor").astype(jnp.float32)
        hidden_state = hidden_state + modulation[:, 2][:, None, :] * branch
        normed = modulate(hidden_state, modulation[:, 3], modulation[:, 4]).astype(jnp.bfloat16)
        hidden_units = jax.nn.gelu(
            rows_product(normed.reshape(req_local * max_len, width), up_weight[layer_at]),
            approximate=True,
        ).astype(jnp.bfloat16)
        branch = cols_product(hidden_units, down_weight[layer_at]).reshape(
            req_local, max_len, width
        )
        branch = lax.psum(branch.astype(jnp.bfloat16), "tensor").astype(jnp.float32)
        hidden_state = hidden_state + modulation[:, 5][:, None, :] * branch
    hidden_state = lax.dynamic_slice_in_dim(hidden_state, own_start, rows_local, 1)
    final_in = modulate(
        hidden_state, mod_full[:, 6 * layer_count], mod_full[:, 6 * layer_count + 1]
    ).astype(jnp.bfloat16)
    noise_own = jnp.einsum(
        "rld,dp->rpl", final_in, output_weight, preferred_element_type=jnp.float32
    )
    return finish(latents, lengths, timesteps, guidance, noise_own, rows_local)


def alpha_table():
    beta_values = np.linspace(0.0001, 0.02, TRAIN_STEPS, dtype=np.float32)
    return np.cumprod(np.float32(1.0) - beta_values, dtype=np.float32)


def finish(latents, lengths, timesteps, guidance, noise_own, rows_local):
    patch_size, max_len = latents.shape[1:]
    guide_at = lax.axis_index("guide")
    is_first = guide_at == 0
    own_start = lax.axis_index("tensor") * rows_local
    own_latents = lax.dynamic_slice_in_dim(latents, own_start, rows_local, 2)
    own_live = (own_start + jnp.arange(rows_local, dtype=jnp.int32))[None, :] < lengths[:, None]
    half_patch = patch_size // 2
    mine_noise = lax.dynamic_slice_in_dim(noise_own, guide_at * half_patch, half_patch, 1)
    other_noise = lax.dynamic_slice_in_dim(noise_own, (1 - guide_at) * half_patch, half_patch, 1)
    partner_noise = from_partner(other_noise, "guide", 0)
    cond_noise = jnp.where(is_first, mine_noise, partner_noise)
    uncond_noise = jnp.where(is_first, partner_noise, mine_noise)
    live_out = own_live[:, None, :]
    guided = uncond_noise + guidance[:, None, None] * (cond_noise - uncond_noise)
    guided = jnp.where(live_out, guided, 0.0)
    half_latents = lax.dynamic_slice_in_dim(own_latents, guide_at * half_patch, half_patch, 1)
    alpha_bar = jnp.asarray(alpha_table())
    step_ids = jnp.arange(TRAIN_STEPS, dtype=jnp.int32)
    alpha_now = jnp.sum(
        jnp.where(step_ids[None, :] == timesteps[:, None], alpha_bar[None, :], 0.0), axis=1
    )[:, None, None]
    alpha_prev = jnp.sum(
        jnp.where(step_ids[None, :] == (timesteps - STRIDE)[:, None], alpha_bar[None, :], 0.0),
        axis=1,
    )[:, None, None]
    start_est = (half_latents - jnp.sqrt(1.0 - alpha_now) * guided) / jnp.sqrt(alpha_now)
    previous = jnp.sqrt(alpha_prev) * start_est + jnp.sqrt(1.0 - alpha_prev) * guided
    previous = jnp.where(live_out, previous, 0.0)
    return (guided, previous)


def exchange(block, axis, bit):
    count = lax.axis_size(axis)
    return lax.ppermute(block, axis, [(at, at ^ bit) for at in range(count)])


HOLDS = {"own": (0,), "two": (4,), "pair": (0, 4), "four": (2, 6)}

PLAN = (
    ((("own", 0),), (("own", 0),)),
    ((("pair", 0),), (("two", 0), ("own", 1))),
    ((("own", 1),), (("four", 0),)),
    ((("pair", 1), ("own", 2)), (("two", 1), ("own", 2), ("own", 3))),
    ((("pair", 2), ("own", 3)), (("four", 1), ("two", 2))),
    ((("pair", 3), ("own", 4)), (("four", 2), ("two", 3))),
    ((("pair", 4), ("own", 5)), (("four", 3), ("pair", 4), ("own", 5))),
    ((("pair", 5),), (("four", 4), ("two", 5))),
    ((), (("four", 5),)),
)
READY = ((0,), (1, 2), (3,), (), (4, 5))


class Stream:
    def __init__(self, make_own):
        self.make_own, self.at = make_own, 0
        self.values, self.arrived, self.sent = {}, {}, ()
        self.blocks = [[] for _ in make_own]

    def hand_over(self, array, parts, flip):
        other = exchange(array, "guide", 1)
        at = 0
        for kind, piece in parts:
            for distance in HOLDS[kind]:
                for which, buffer in enumerate((array, other)):
                    self.blocks[piece].append((buffer, at, distance ^ flip, which))
                at += 1

    def step(self, *first):
        over_z, over_x = PLAN[self.at] if self.at < len(PLAN) else ((), ())
        for piece in READY[self.at] if self.at < len(READY) else ():
            self.values["own", piece] = self.make_own[piece]()
        self.at += 1
        self.values, arrived, _ = lax.optimization_barrier((self.values, self.arrived, first))
        self.values = values = dict(self.values)
        for (kind, piece), value in arrived.items():
            if kind == "own":
                values["two", piece] = value
                values["pair", piece] = jnp.concatenate([values["own", piece], value], axis=0)
            elif kind == "pair":
                values["four", piece] = value
        self.arrived = {}
        source = [values[part] for part in over_x]
        if source:
            source = source[0] if len(source) == 1 else jnp.concatenate(source, axis=0)
            self.arrived["x", ""] = exchange(source, "batch", 1)
        for kind, piece in over_z:
            bit = 4 if kind == "own" else 2
            self.arrived[kind, piece] = exchange(values[kind, piece], "batch", bit)
        if ("x", "") in arrived:
            self.hand_over(arrived["x", ""], self.sent, 1)
        if over_x:
            self.hand_over(source, over_x, 0)
        self.sent = over_x

    def operands(self, piece):
        arrays, places = [], []
        for buffer, at, distance, which in self.blocks[piece]:
            found = [n for n, array in enumerate(arrays) if array is buffer]
            if not found:
                arrays.append(buffer)
            places.append((found[0] if found else len(arrays) - 1, at, distance, which))
        return arrays, places


def fetch(weights, slots, buffers, places, batch_at, arrivals):
    rows = weights.shape[1] // (len(places) // 2)
    copies = []
    for number, (array, at, distance, which) in enumerate(places):
        row = pl.multiple_of((batch_at ^ distance) * rows, 16)
        copies.append(
            pltpu.make_async_copy(
                buffers[array].at[pl.ds(at * rows, rows), :],
                weights.at[slots[which], pl.ds(row, rows), :],
                arrivals.at[number],
            )
        )
        copies[-1].start()
    return copies


def normalized(hidden, shift, scale):
    center = hidden - jnp.mean(hidden, axis=-1, keepdims=True)
    spread = jnp.mean(center * center, axis=-1, keepdims=True)
    return center * lax.rsqrt(spread + norm_epsilon) * (1.0 + scale) + shift


def dot_nt(left, right):
    return lax.dot_general(
        left, right, (((1,), (1,)), ((), ())), preferred_element_type=jnp.float32
    )


def kernel_call(body, outs, scratch, operands, buffers, fetches, flops, bytes_moved):
    specs = [pl.BlockSpec(memory_space=pltpu.SMEM)]
    specs += [pl.BlockSpec(memory_space=pltpu.VMEM) for _ in operands[1:]]
    specs += [pl.BlockSpec(memory_space=pl.ANY) for _ in buffers]
    scratch = scratch + [pltpu.SemaphoreType.DMA((16,))] * fetches
    return pl.pallas_call(
        body,
        out_shape=outs,
        in_specs=specs,
        out_specs=jax.tree.map(lambda _: pl.BlockSpec(memory_space=pltpu.VMEM), outs),
        scratch_shapes=scratch,
        cost_estimate=pl.CostEstimate(
            flops=int(flops), bytes_accessed=int(bytes_moved), transcendentals=0
        ),
        compiler_params=pltpu.CompilerParams(vmem_limit_bytes=44 * 2**20),
    )(*operands, *buffers)


def enter(hidden, branches, mods, row, hidden_out, normed, first_row=0):
    state = hidden[pl.ds(first_row, normed.shape[0]), :]
    if branches:
        total = branches[0][...].astype(jnp.float32) + branches[1][...].astype(jnp.float32)
        state = state + mods[row - 1 : row, :] * total
        if hidden_out is not None:
            hidden_out[...] = state
    normed[...] = normalized(state, mods[row : row + 1, :], mods[row + 1 : row + 2, :]).astype(
        jnp.bfloat16
    )


def attention_kernel(places, array_count, layer, heads, branch_count, ids, hidden, mods, *refs):
    branches, refs = refs[:branch_count], refs[branch_count:]
    buffers, refs = refs[:array_count], refs[array_count:]
    hidden_out = other_half = None
    if branches:
        hidden_out, other_half, refs = refs[0], refs[1], refs[2:]
    partial, weights, normed, projected, split, attended, arrivals = refs
    width, keys = hidden.shape[1], hidden.shape[0]
    half = width // 2
    copies = fetch(weights, [ids[1], 1 - ids[1]], buffers, places, ids[0], arrivals)
    enter(hidden, branches, mods, 6 * layer, hidden_out, normed)
    for copy in copies:
        copy.wait()

    def step(at, carry):
        lo = pl.multiple_of(at * 384, 128)
        projected[:, pl.ds(lo, 384)] = jnp.dot(
            normed[...], weights[0, :, pl.ds(lo, 384)], preferred_element_type=jnp.float32
        ).astype(jnp.bfloat16)
        return carry

    lax.fori_loop(0, width // 384, step, 0)
    projected[:, width:] = jnp.dot(
        normed[...], weights[1, :, :half], preferred_element_type=jnp.float32
    ).astype(jnp.bfloat16)
    for at in range(3 * heads):
        split[at] = projected[:, at * HDIM : (at + 1) * HDIM]
    factor = math.log2(math.e) / math.sqrt(HDIM)
    live = lax.broadcasted_iota(jnp.int32, (1, keys), 1) < ids[3]
    for at in range(heads):
        scores = dot_nt(split[at], split[heads + at])
        scores = jnp.where(live, scores * factor, -jnp.inf)
        raised = jnp.exp2(scores - jnp.max(scores, axis=-1, keepdims=True))
        total = jnp.sum(raised, axis=-1, keepdims=True)
        out = jnp.dot(
            raised.astype(jnp.bfloat16), split[2 * heads + at], preferred_element_type=jnp.float32
        )
        attended[:, at * HDIM : (at + 1) * HDIM] = (out / total).astype(jnp.bfloat16)
    proj = weights[1, :, half:]
    if other_half is None:
        partial[...] = dot_nt(attended[...], proj).astype(jnp.bfloat16)
    else:
        rows = partial.shape[0]
        for out, which in ((partial, ids[2]), (other_half, 1 - ids[2])):
            some = attended[pl.ds(pl.multiple_of(which * rows, 16), rows), :]
            out[...] = dot_nt(some, proj).astype(jnp.bfloat16)


def expand(normed, weights, units):
    width = normed.shape[1]
    for half in range(2):

        def step(at, carry):
            lo = pl.multiple_of(at * 384, 128)
            product = jnp.dot(
                normed[...], weights[half, :, pl.ds(lo, 384)], preferred_element_type=jnp.float32
            )
            inner = math.sqrt(2.0 / math.pi) * (product + 0.044715 * product * product * product)
            units[half, :, pl.ds(lo, 384)] = (0.5 * product * (1.0 + jnp.tanh(inner))).astype(
                jnp.bfloat16
            )
            return carry

        lax.fori_loop(0, width // 384, step, 0)


def contract(units, weights, partial):
    width = partial.shape[1]

    def step(at, carry):
        lo = pl.multiple_of(at * 384, 128)
        product = dot_nt(units[0], weights[0, pl.ds(lo, 384), :])
        product = product + dot_nt(units[1], weights[1, pl.ds(lo, 384), :])
        partial[:, pl.ds(lo, 384)] = product.astype(jnp.bfloat16)
        return carry

    lax.fori_loop(0, width // 384, step, 0)


def up_kernel(places, array_count, layer, ids, hidden, mods, *refs):
    branches, refs = refs[:2], refs[2:]
    buffers, refs = refs[:array_count], refs[array_count:]
    hidden_out, units, weights, normed, arrivals = refs
    copies = fetch(weights, [0, 1], buffers, places, ids[0], arrivals)
    enter(hidden, branches, mods, 6 * layer + 3, hidden_out, normed)
    for copy in copies:
        copy.wait()
    expand(normed, weights, units)


def down_kernel(places, array_count, ids, units, *refs):
    buffers, (partial, weights, arrivals) = refs[:array_count], refs[array_count:]
    for copy in fetch(weights, [0, 1], buffers, places, ids[0], arrivals):
        copy.wait()
    contract(units, weights, partial)


def mlp_kernel(places, counts, layer, own, ids, hidden, mods, *refs):
    branches, refs = refs[:2], refs[2:]
    ups, downs, refs = refs[: counts[0]], refs[counts[0] : sum(counts)], refs[sum(counts) :]
    hidden_out = None
    if own:
        hidden_out, refs = refs[0], refs[1:]
    partial, up_weights, down_weights, units, normed, arrivals, more_arrivals = refs
    rows = partial.shape[0]
    first_row = pl.multiple_of((ids[2] if own else 1 - ids[2]) * rows, 16)
    up_copies = fetch(up_weights, [0, 1], ups, places[0], ids[0], arrivals)
    down_copies = fetch(down_weights, [0, 1], downs, places[1], ids[0], more_arrivals)
    enter(hidden, branches, mods, 6 * layer + 3, hidden_out, normed, first_row)
    for copy in up_copies:
        copy.wait()
    expand(normed, up_weights, units)
    for copy in down_copies:
        copy.wait()
    contract(units, down_weights, partial)


def modulation_sums(columns, modulation_weight, final_modulation):
    layer_count, _, _, head_cols = modulation_weight.shape
    blocks = jnp.einsum(
        "rk,lkjc->rljc", columns, modulation_weight, preferred_element_type=jnp.float32
    ).reshape(columns.shape[0], 6 * layer_count, head_cols)
    finals = jnp.einsum("rk,kjc->rjc", columns, final_modulation, preferred_element_type=jnp.float32)
    return jnp.concatenate([blocks, finals], axis=1)


def all_columns(mine):
    other = exchange(mine, "tensor", 1)
    first = lax.axis_index("tensor") == 0
    return jnp.concatenate(
        [jnp.where(first, mine, other), jnp.where(first, other, mine)], axis=1
    )


def fast_local(
    latents,
    lengths,
    timesteps,
    guidance,
    condition,
    embed_weight,
    modulation_weight,
    final_modulation,
    qkv_weight,
    proj_weight,
    up_weight,
    down_weight,
    output_weight,
):
    tensor_at = lax.axis_index("tensor")
    batch_at = lax.axis_index("batch")
    guide_at = lax.axis_index("guide")
    _, patch_size, max_len = latents.shape
    width = embed_weight.shape[1]
    half = width // 2
    layer_count = qkv_weight.shape[0]
    heads = half // HDIM
    rows_own = max_len // 2
    width_piece = qkv_weight.shape[1]
    first = guide_at == 0
    ids = jnp.stack([batch_at, guide_at, tensor_at, lengths[0]]).astype(jnp.int32)
    bf16, f32 = jnp.bfloat16, jnp.float32

    def attention_piece(layer):
        queries_keys = qkv_weight[layer, :, :2].reshape(width_piece, width)
        values_proj = jnp.concatenate([qkv_weight[layer, :, 2], proj_weight[layer].T], axis=1)
        return jnp.where(first, queries_keys, values_proj)

    def up_piece(layer):
        return lax.dynamic_slice_in_dim(up_weight[layer], guide_at * width, width, 1)

    def down_piece(layer):
        return lax.dynamic_slice_in_dim(down_weight[layer], guide_at * width, width, 0).T

    stream = Stream(
        [
            functools.partial(make, layer)
            for layer in range(layer_count)
            for make in (attention_piece, up_piece, down_piece)
        ]
    )
    weight_bytes = 4 * width * width
    shape = jax.ShapeDtypeStruct
    two_weights = pltpu.VMEM((2, width, width), bf16)
    normed = pltpu.VMEM((max_len, width), bf16)

    def attention_block(layer, hidden, mods, branches):
        outs = [shape((max_len, width), bf16)]
        if branches:
            outs = [shape((max_len, width), f32)] + [shape((rows_own, width), bf16)] * 2
        arrays, places = stream.operands(3 * layer)
        results = kernel_call(
            functools.partial(attention_kernel, places, len(arrays), layer, heads, len(branches)),
            outs,
            [
                two_weights,
                normed,
                pltpu.VMEM((max_len, 3 * half), bf16),
                pltpu.VMEM((3 * heads, max_len, HDIM), bf16),
                pltpu.VMEM((max_len, half), bf16),
            ],
            [ids, hidden, mods, *branches],
            arrays,
            1,
            2 * max_len * width * 4 * half + 4 * max_len * max_len * half,
            weight_bytes,
        )
        return results if branches else results[0]

    def both(partial):
        return [partial, exchange(partial, "tensor", 1)]

    def up_block(layer, hidden, mods, branches):
        arrays, places = stream.operands(3 * layer + 1)
        return kernel_call(
            functools.partial(up_kernel, places, len(arrays), layer),
            [shape((max_len, width), f32), shape((2, max_len, width), bf16)],
            [two_weights, normed],
            [ids, hidden, mods, *branches],
            arrays,
            1,
            4 * max_len * width * width,
            weight_bytes,
        )

    def down_block(layer, units):
        arrays, places = stream.operands(3 * layer + 2)
        return kernel_call(
            functools.partial(down_kernel, places, len(arrays)),
            shape((max_len, width), bf16),
            [two_weights],
            [ids, units],
            arrays,
            1,
            4 * max_len * width * width,
            weight_bytes,
        )

    def mlp_block(layer, own, hidden, mods, branches):
        arrays, places = stream.operands(3 * layer + 1)
        more_arrays, more_places = stream.operands(3 * layer + 2)
        counts = (len(arrays), len(more_arrays))
        return kernel_call(
            functools.partial(mlp_kernel, (places, more_places), counts, layer, own),
            [shape((rows_own, width), f32)] * own + [shape((rows_own, width), bf16)],
            [
                two_weights,
                two_weights,
                pltpu.VMEM((2, rows_own, width), bf16),
                pltpu.VMEM((rows_own, width), bf16),
            ],
            [ids, hidden, mods, *branches],
            arrays + more_arrays,
            2,
            8 * rows_own * width * width,
            2 * weight_bytes,
        )

    activated = jax.nn.silu(condition[0]).astype(bf16).reshape(-1, width_piece)
    stream.step()
    columns = lax.all_to_all(activated, "batch", 0, 0, tiled=True)
    stream.step(columns)
    sums = modulation_sums(columns, modulation_weight, final_modulation)
    mine = jnp.sum(lax.all_to_all(sums, "batch", 0, 0, tiled=True), axis=0)
    hidden = jnp.einsum(
        "pl,pd->ld", latents[0], embed_weight, precision=lax.Precision.HIGHEST
    ) + jnp.asarray(position_values(max_len, width))
    stream.step(mine, hidden)
    mods = all_columns(mine)
    stream.step(mods)
    partial = attention_block(0, hidden, mods, [])
    stream.step(partial)
    branches = both(partial)
    stream.step(branches)
    hidden, units = up_block(0, hidden, mods, branches)
    stream.step(units)
    branches = both(down_block(0, units))
    stream.step(branches)
    hidden, other_half, own_half = attention_block(1, hidden, mods, branches)
    stream.step(other_half, own_half)
    for_other = exchange(own_half, "tensor", 1)
    for_own = exchange(other_half, "tensor", 1)
    stream.step(for_other)
    (sent,) = mlp_block(1, False, hidden, mods, [other_half, for_other])
    theirs = exchange(sent, "tensor", 1)
    hidden, mine = mlp_block(1, True, hidden, mods, [own_half, for_own])
    hidden = hidden + mods[6 * layer_count - 1][None, :] * (
        mine.astype(f32) + theirs.astype(f32)
    )
    final_in = normalized(
        hidden, mods[6 * layer_count][None, :], mods[6 * layer_count + 1][None, :]
    ).astype(bf16)
    noise_own = lax.dot_general(
        output_weight, final_in, (((0,), (1,)), ((), ())), preferred_element_type=f32
    )[None]
    return finish(latents, lengths, timesteps, guidance, noise_own, rows_own)


def solution(mesh):
    in_specs = (
        P("batch", None, None),
        P("batch"),
        P("batch"),
        P("batch"),
        P("guide", "batch", None),
        P(),
        P(None, "batch", None, "tensor"),
        P("batch", None, "tensor"),
        P(None, "batch", None, "tensor"),
        P(None, "tensor", "batch"),
        P(None, "batch", "tensor"),
        P(None, "tensor", "batch"),
        P(),
    )
    out_specs = (P("batch", "guide", "tensor"), P("batch", "guide", "tensor"))
    sizes = mesh.shape
    small = sizes["batch"] == 8 and sizes["tensor"] == 2
    body = fast_local if small else local
    return jax.shard_map(body, mesh=mesh, in_specs=in_specs, out_specs=out_specs, check_vma=False)
```

```python
import functools
import math

import jax
import jax.numpy as jnp
import numpy as np
from jax import lax
from jax.experimental import pallas as pl
from jax.experimental.pallas import tpu as pltpu
from jax.sharding import PartitionSpec as P

HDIM = 72
TRAIN_STEPS = 1000
STRIDE = 20


norm_epsilon = 1e-06


def from_partner(block, axis, distance):
    count = lax.axis_size(axis)
    route = []
    for low in range(count):
        high = low | 1 << distance
        if high != low and high < count:
            route += [(low, high), (high, low)]
    return lax.ppermute(block, axis, route)


def layer_norm(values):
    center = values - jnp.mean(values, axis=-1, keepdims=True)
    spread = jnp.mean(center * center, axis=-1, keepdims=True)
    return center * lax.rsqrt(spread + norm_epsilon)


def modulate(values, shift, scale):
    return layer_norm(values) * (1.0 + scale[:, None, :]) + shift[:, None, :]


def position_values(row_count, width):
    half_width = width // 2
    frequency = np.exp(
        np.arange(half_width, dtype=np.float32) * np.float32(-math.log(10000.0) / half_width)
    )
    angles = np.arange(row_count, dtype=np.float32)[:, None] * frequency[None, :]
    return np.concatenate([np.sin(angles), np.cos(angles)], axis=1).astype(np.float32)


def position_table(row_count, width):
    rows_at = jnp.arange(row_count, dtype=jnp.int32).astype(jnp.float32)
    half_width = width // 2
    frequency = jnp.exp(
        jnp.arange(half_width, dtype=jnp.float32) * (-math.log(10000.0) / half_width)
    )
    angles = rows_at[:, None] * frequency[None, :]
    return jnp.concatenate([jnp.sin(angles), jnp.cos(angles)], axis=1)


def attend(operands):
    projected_item, key_live = operands
    score_scale = 1.0 / math.sqrt(HDIM)
    scores = (
        jnp.einsum(
            "qhd,khd->hqk",
            projected_item[:, 0],
            projected_item[:, 1],
            preferred_element_type=jnp.float32,
        )
        * score_scale
    )
    scores = jnp.where(key_live[None, None, :], scores, -jnp.inf)
    row_max = jnp.max(scores, axis=-1, keepdims=True)
    exp_scores = jnp.exp(scores - row_max)
    probabilities = (exp_scores / jnp.sum(exp_scores, axis=-1, keepdims=True)).astype(jnp.bfloat16)
    attended = jnp.einsum(
        "hqk,khd->qhd", probabilities, projected_item[:, 2], preferred_element_type=jnp.float32
    )
    return attended.astype(jnp.bfloat16).reshape(
        attended.shape[0], attended.shape[1] * attended.shape[2]
    )


def local(
    latents,
    lengths,
    timesteps,
    guidance,
    condition,
    embed_weight,
    modulation_weight,
    final_modulation,
    qkv_weight,
    proj_weight,
    up_weight,
    down_weight,
    output_weight,
):
    tensor_count = lax.axis_size("tensor")
    batch_count = lax.axis_size("batch")
    tensor_at = lax.axis_index("tensor")
    batch_at = lax.axis_index("batch")
    req_local, patch_size, max_len = latents.shape
    width = embed_weight.shape[1]
    layer_count = qkv_weight.shape[0]
    head_cols = qkv_weight.shape[3]
    heads_local = head_cols // HDIM
    rows_local = max_len // tensor_count
    width_piece = width // batch_count
    mod_count = 6 * layer_count + 2

    def rows_product(activation, shard):
        return jnp.dot(
            activation,
            lax.all_gather(shard, "batch", axis=0, tiled=True),
            preferred_element_type=jnp.float32,
        )

    def cols_product(activation, shard):
        return jnp.dot(
            activation,
            lax.all_gather(shard, "batch", axis=1, tiled=True),
            preferred_element_type=jnp.float32,
        )

    cond_act = jax.nn.silu(condition[0]).astype(jnp.bfloat16)
    cond_all = lax.all_gather(cond_act, "batch", axis=0, tiled=True)
    cond_cols = lax.dynamic_slice_in_dim(cond_all, batch_at * width_piece, width_piece, 1)
    block_local = jnp.transpose(modulation_weight, (1, 0, 2, 3)).reshape(
        width_piece, 6 * layer_count * head_cols
    )
    mod_local = jnp.concatenate(
        [block_local, final_modulation.reshape(width_piece, 2 * head_cols)], axis=1
    )
    mod_mine = lax.psum_scatter(
        jnp.dot(cond_cols, mod_local, preferred_element_type=jnp.float32),
        "batch",
        scatter_dimension=0,
        tiled=True,
    )
    mod_full = lax.all_gather(
        mod_mine.reshape(req_local, mod_count, head_cols), "tensor", axis=2, tiled=True
    )
    positions = jnp.arange(max_len, dtype=jnp.int32)
    live_mask = positions[None, :] < lengths[:, None]
    own_start = tensor_at * rows_local
    hidden_state = (
        jnp.einsum("rpl,pd->rld", latents, embed_weight, precision=lax.Precision.HIGHEST)
        + position_table(max_len, width)[None]
    )
    for layer_at in range(layer_count):
        modulation = mod_full[:, 6 * layer_at : 6 * layer_at + 6]
        normed = modulate(hidden_state, modulation[:, 0], modulation[:, 1]).astype(jnp.bfloat16)
        projected = rows_product(
            normed.reshape(req_local * max_len, width),
            qkv_weight[layer_at].reshape(width_piece, 3 * head_cols),
        ).astype(jnp.bfloat16)
        projected = projected.reshape(req_local, max_len, 3, heads_local, HDIM)
        attended = lax.map(attend, (projected, live_mask))
        branch = cols_product(
            attended.reshape(req_local * max_len, head_cols), proj_weight[layer_at]
        ).reshape(req_local, max_len, width)
        branch = lax.psum(branch.astype(jnp.bfloat16), "tensor").astype(jnp.float32)
        hidden_state = hidden_state + modulation[:, 2][:, None, :] * branch
        normed = modulate(hidden_state, modulation[:, 3], modulation[:, 4]).astype(jnp.bfloat16)
        hidden_units = jax.nn.gelu(
            rows_product(normed.reshape(req_local * max_len, width), up_weight[layer_at]),
            approximate=True,
        ).astype(jnp.bfloat16)
        branch = cols_product(hidden_units, down_weight[layer_at]).reshape(
            req_local, max_len, width
        )
        branch = lax.psum(branch.astype(jnp.bfloat16), "tensor").astype(jnp.float32)
        hidden_state = hidden_state + modulation[:, 5][:, None, :] * branch
    hidden_state = lax.dynamic_slice_in_dim(hidden_state, own_start, rows_local, 1)
    final_in = modulate(
        hidden_state, mod_full[:, 6 * layer_count], mod_full[:, 6 * layer_count + 1]
    ).astype(jnp.bfloat16)
    noise_own = jnp.einsum(
        "rld,dp->rpl", final_in, output_weight, preferred_element_type=jnp.float32
    )
    return finish(latents, lengths, timesteps, guidance, noise_own, rows_local)


def alpha_table():
    beta_values = np.linspace(0.0001, 0.02, TRAIN_STEPS, dtype=np.float32)
    return np.cumprod(np.float32(1.0) - beta_values, dtype=np.float32)


def finish(latents, lengths, timesteps, guidance, noise_own, rows_local):
    patch_size, max_len = latents.shape[1:]
    guide_at = lax.axis_index("guide")
    is_first = guide_at == 0
    own_start = lax.axis_index("tensor") * rows_local
    own_latents = lax.dynamic_slice_in_dim(latents, own_start, rows_local, 2)
    own_live = (own_start + jnp.arange(rows_local, dtype=jnp.int32))[None, :] < lengths[:, None]
    half_patch = patch_size // 2
    mine_noise = lax.dynamic_slice_in_dim(noise_own, guide_at * half_patch, half_patch, 1)
    other_noise = lax.dynamic_slice_in_dim(noise_own, (1 - guide_at) * half_patch, half_patch, 1)
    partner_noise = from_partner(other_noise, "guide", 0)
    cond_noise = jnp.where(is_first, mine_noise, partner_noise)
    uncond_noise = jnp.where(is_first, partner_noise, mine_noise)
    live_out = own_live[:, None, :]
    guided = uncond_noise + guidance[:, None, None] * (cond_noise - uncond_noise)
    guided = jnp.where(live_out, guided, 0.0)
    half_latents = lax.dynamic_slice_in_dim(own_latents, guide_at * half_patch, half_patch, 1)
    alpha_bar = jnp.asarray(alpha_table())
    step_ids = jnp.arange(TRAIN_STEPS, dtype=jnp.int32)
    alpha_now = jnp.sum(
        jnp.where(step_ids[None, :] == timesteps[:, None], alpha_bar[None, :], 0.0), axis=1
    )[:, None, None]
    alpha_prev = jnp.sum(
        jnp.where(step_ids[None, :] == (timesteps - STRIDE)[:, None], alpha_bar[None, :], 0.0),
        axis=1,
    )[:, None, None]
    start_est = (half_latents - jnp.sqrt(1.0 - alpha_now) * guided) / jnp.sqrt(alpha_now)
    previous = jnp.sqrt(alpha_prev) * start_est + jnp.sqrt(1.0 - alpha_prev) * guided
    previous = jnp.where(live_out, previous, 0.0)
    return (guided, previous)


def exchange(block, axis, bit):
    count = lax.axis_size(axis)
    return lax.ppermute(block, axis, [(at, at ^ bit) for at in range(count)])


HOLDS = {"own": (0,), "two": (4,), "pair": (0, 4), "four": (2, 6)}

PLAN = (
    ((("own", 0),), (("own", 0),)),
    ((("pair", 0),), (("two", 0), ("own", 1))),
    ((("own", 1),), (("four", 0),)),
    ((("pair", 1), ("own", 2)), (("two", 1), ("own", 2), ("own", 3))),
    ((("pair", 2), ("own", 3)), (("four", 1), ("two", 2))),
    ((("pair", 3), ("own", 4)), (("four", 2), ("two", 3))),
    ((("pair", 4), ("own", 5)), (("four", 3), ("pair", 4), ("own", 5))),
    ((("pair", 5),), (("four", 4), ("two", 5))),
    ((), (("four", 5),)),
)
READY = ((0,), (1, 2), (3,), (), (4, 5))


class Stream:
    def __init__(self, make_own):
        self.make_own, self.at = make_own, 0
        self.values, self.arrived, self.sent = {}, {}, ()
        self.blocks = [[] for _ in make_own]

    def hand_over(self, array, parts, flip):
        other = exchange(array, "guide", 1)
        at = 0
        for kind, piece in parts:
            for distance in HOLDS[kind]:
                for which, buffer in enumerate((array, other)):
                    self.blocks[piece].append((buffer, at, distance ^ flip, which))
                at += 1

    def step(self, *first):
        over_z, over_x = PLAN[self.at] if self.at < len(PLAN) else ((), ())
        for piece in READY[self.at] if self.at < len(READY) else ():
            self.values["own", piece] = self.make_own[piece]()
        self.at += 1
        self.values, arrived, _ = lax.optimization_barrier((self.values, self.arrived, first))
        self.values = values = dict(self.values)
        for (kind, piece), value in arrived.items():
            if kind == "own":
                values["two", piece] = value
                values["pair", piece] = jnp.concatenate([values["own", piece], value], axis=0)
            elif kind == "pair":
                values["four", piece] = value
        self.arrived = {}
        source = [values[part] for part in over_x]
        if source:
            source = source[0] if len(source) == 1 else jnp.concatenate(source, axis=0)
            self.arrived["x", ""] = exchange(source, "batch", 1)
        for kind, piece in over_z:
            bit = 4 if kind == "own" else 2
            self.arrived[kind, piece] = exchange(values[kind, piece], "batch", bit)
        if ("x", "") in arrived:
            self.hand_over(arrived["x", ""], self.sent, 1)
        if over_x:
            self.hand_over(source, over_x, 0)
        self.sent = over_x

    def operands(self, piece):
        arrays, places = [], []
        for buffer, at, distance, which in self.blocks[piece]:
            found = [n for n, array in enumerate(arrays) if array is buffer]
            if not found:
                arrays.append(buffer)
            places.append((found[0] if found else len(arrays) - 1, at, distance, which))
        return arrays, places


def fetch(weights, slots, buffers, places, batch_at, arrivals):
    rows = weights.shape[1] // (len(places) // 2)
    copies = []
    for number, (array, at, distance, which) in enumerate(places):
        row = pl.multiple_of((batch_at ^ distance) * rows, 16)
        copies.append(
            pltpu.make_async_copy(
                buffers[array].at[pl.ds(at * rows, rows), :],
                weights.at[slots[which], pl.ds(row, rows), :],
                arrivals.at[number],
            )
        )
        copies[-1].start()
    return copies


def normalized(hidden, shift, scale):
    center = hidden - jnp.mean(hidden, axis=-1, keepdims=True)
    spread = jnp.mean(center * center, axis=-1, keepdims=True)
    return center * lax.rsqrt(spread + norm_epsilon) * (1.0 + scale) + shift


def dot_nt(left, right):
    return lax.dot_general(
        left, right, (((1,), (1,)), ((), ())), preferred_element_type=jnp.float32
    )


def kernel_call(body, outs, scratch, operands, buffers, fetches, flops, bytes_moved, mib=44):
    specs = [pl.BlockSpec(memory_space=pltpu.SMEM)]
    specs += [pl.BlockSpec(memory_space=pltpu.VMEM) for _ in operands[1:]]
    specs += [pl.BlockSpec(memory_space=pl.ANY) for _ in buffers]
    scratch = scratch + [pltpu.SemaphoreType.DMA((16,))] * fetches
    return pl.pallas_call(
        body,
        out_shape=outs,
        in_specs=specs,
        out_specs=jax.tree.map(lambda _: pl.BlockSpec(memory_space=pltpu.VMEM), outs),
        scratch_shapes=scratch,
        cost_estimate=pl.CostEstimate(
            flops=int(flops), bytes_accessed=int(bytes_moved), transcendentals=0
        ),
        compiler_params=pltpu.CompilerParams(vmem_limit_bytes=mib * 2**20),
    )(*operands, *buffers)


def enter(hidden, branches, mods, row, hidden_out, normed, first_row=0):
    state = hidden[pl.ds(first_row, normed.shape[0]), :]
    if branches:
        total = branches[0][...].astype(jnp.float32) + branches[1][...].astype(jnp.float32)
        state = state + mods[row - 1 : row, :] * total
        if hidden_out is not None:
            hidden_out[...] = state
    normed[...] = normalized(state, mods[row : row + 1, :], mods[row + 1 : row + 2, :]).astype(
        jnp.bfloat16
    )


def attention_kernel(places, array_count, layer, heads, branch_count, ids, hidden, mods, *refs):
    branches, refs = refs[:branch_count], refs[branch_count:]
    buffers, refs = refs[:array_count], refs[array_count:]
    hidden_out = other_half = None
    if branches:
        hidden_out, other_half, refs = refs[0], refs[1], refs[2:]
    partial, weights, normed, projected, split, attended, arrivals = refs
    width, keys = hidden.shape[1], hidden.shape[0]
    half = width // 2
    copies = fetch(weights, [ids[1], 1 - ids[1]], buffers, places, ids[0], arrivals)
    enter(hidden, branches, mods, 6 * layer, hidden_out, normed)
    for copy in copies:
        copy.wait()

    def step(at, carry):
        lo = pl.multiple_of(at * 384, 128)
        projected[:, pl.ds(lo, 384)] = jnp.dot(
            normed[...], weights[0, :, pl.ds(lo, 384)], preferred_element_type=jnp.float32
        ).astype(jnp.bfloat16)
        return carry

    lax.fori_loop(0, width // 384, step, 0)
    projected[:, width:] = jnp.dot(
        normed[...], weights[1, :, :half], preferred_element_type=jnp.float32
    ).astype(jnp.bfloat16)
    for at in range(3 * heads):
        split[at] = projected[:, at * HDIM : (at + 1) * HDIM]
    factor = math.log2(math.e) / math.sqrt(HDIM)
    live = lax.broadcasted_iota(jnp.int32, (1, keys), 1) < ids[3]
    for at in range(heads):
        scores = dot_nt(split[at], split[heads + at])
        scores = jnp.where(live, scores * factor, -jnp.inf)
        raised = jnp.exp2(scores - jnp.max(scores, axis=-1, keepdims=True))
        total = jnp.sum(raised, axis=-1, keepdims=True)
        out = jnp.dot(
            raised.astype(jnp.bfloat16), split[2 * heads + at], preferred_element_type=jnp.float32
        )
        attended[:, at * HDIM : (at + 1) * HDIM] = (out / total).astype(jnp.bfloat16)
    proj = weights[1, :, half:]
    if other_half is None:
        partial[...] = dot_nt(attended[...], proj).astype(jnp.bfloat16)
    else:
        rows = partial.shape[0]
        for out, which in ((partial, ids[2]), (other_half, 1 - ids[2])):
            some = attended[pl.ds(pl.multiple_of(which * rows, 16), rows), :]
            out[...] = dot_nt(some, proj).astype(jnp.bfloat16)


def expand(normed, weights, units):
    width = normed.shape[1]
    for half in range(2):

        def step(at, carry):
            lo = pl.multiple_of(at * 384, 128)
            product = jnp.dot(
                normed[...], weights[half, :, pl.ds(lo, 384)], preferred_element_type=jnp.float32
            )
            inner = math.sqrt(2.0 / math.pi) * (product + 0.044715 * product * product * product)
            units[half, :, pl.ds(lo, 384)] = (0.5 * product * (1.0 + jnp.tanh(inner))).astype(
                jnp.bfloat16
            )
            return carry

        lax.fori_loop(0, width // 384, step, 0)


def contract(units, weights, partial):
    width = partial.shape[1]

    def step(at, carry):
        lo = pl.multiple_of(at * 384, 128)
        product = dot_nt(units[0], weights[0, pl.ds(lo, 384), :])
        product = product + dot_nt(units[1], weights[1, pl.ds(lo, 384), :])
        partial[:, pl.ds(lo, 384)] = product.astype(jnp.bfloat16)
        return carry

    lax.fori_loop(0, width // 384, step, 0)


def up_kernel(places, array_count, layer, ids, hidden, mods, *refs):
    branches, refs = refs[:2], refs[2:]
    buffers, refs = refs[:array_count], refs[array_count:]
    hidden_out, units, weights, normed, arrivals = refs
    copies = fetch(weights, [0, 1], buffers, places, ids[0], arrivals)
    enter(hidden, branches, mods, 6 * layer + 3, hidden_out, normed)
    for copy in copies:
        copy.wait()
    expand(normed, weights, units)


def down_kernel(places, array_count, ids, units, *refs):
    buffers, (partial, weights, arrivals) = refs[:array_count], refs[array_count:]
    for copy in fetch(weights, [0, 1], buffers, places, ids[0], arrivals):
        copy.wait()
    contract(units, weights, partial)


def mlp_kernel(places, counts, layer, own, ids, hidden, mods, *refs):
    branches, refs = refs[:2], refs[2:]
    ups, downs, refs = refs[: counts[0]], refs[counts[0] : sum(counts)], refs[sum(counts) :]
    hidden_out = None
    if own:
        hidden_out, refs = refs[0], refs[1:]
    partial, up_weights, down_weights, units, normed, arrivals, more_arrivals = refs
    rows = partial.shape[0]
    first_row = pl.multiple_of((ids[2] if own else 1 - ids[2]) * rows, 16)
    up_copies = fetch(up_weights, [0, 1], ups, places[0], ids[0], arrivals)
    down_copies = fetch(down_weights, [0, 1], downs, places[1], ids[0], more_arrivals)
    enter(hidden, branches, mods, 6 * layer + 3, hidden_out, normed, first_row)
    for copy in up_copies:
        copy.wait()
    expand(normed, up_weights, units)
    for copy in down_copies:
        copy.wait()
    contract(units, down_weights, partial)


def modulation_sums(columns, modulation_weight, final_modulation):
    layer_count, _, _, head_cols = modulation_weight.shape
    blocks = jnp.einsum(
        "rk,lkjc->rljc", columns, modulation_weight, preferred_element_type=jnp.float32
    ).reshape(columns.shape[0], 6 * layer_count, head_cols)
    finals = jnp.einsum("rk,kjc->rjc", columns, final_modulation, preferred_element_type=jnp.float32)
    return jnp.concatenate([blocks, finals], axis=1)


def all_columns(mine):
    other = exchange(mine, "tensor", 1)
    first = lax.axis_index("tensor") == 0
    return jnp.concatenate(
        [jnp.where(first, mine, other), jnp.where(first, other, mine)], axis=1
    )


def fast_local(
    latents,
    lengths,
    timesteps,
    guidance,
    condition,
    embed_weight,
    modulation_weight,
    final_modulation,
    qkv_weight,
    proj_weight,
    up_weight,
    down_weight,
    output_weight,
):
    tensor_at = lax.axis_index("tensor")
    batch_at = lax.axis_index("batch")
    guide_at = lax.axis_index("guide")
    _, patch_size, max_len = latents.shape
    width = embed_weight.shape[1]
    half = width // 2
    layer_count = qkv_weight.shape[0]
    heads = half // HDIM
    rows_own = max_len // 2
    width_piece = qkv_weight.shape[1]
    first = guide_at == 0
    ids = jnp.stack([batch_at, guide_at, tensor_at, lengths[0]]).astype(jnp.int32)
    bf16, f32 = jnp.bfloat16, jnp.float32

    def attention_piece(layer):
        queries_keys = qkv_weight[layer, :, :2].reshape(width_piece, width)
        values_proj = jnp.concatenate([qkv_weight[layer, :, 2], proj_weight[layer].T], axis=1)
        return jnp.where(first, queries_keys, values_proj)

    def up_piece(layer):
        return lax.dynamic_slice_in_dim(up_weight[layer], guide_at * width, width, 1)

    def down_piece(layer):
        return lax.dynamic_slice_in_dim(down_weight[layer], guide_at * width, width, 0).T

    stream = Stream(
        [
            functools.partial(make, layer)
            for layer in range(layer_count)
            for make in (attention_piece, up_piece, down_piece)
        ]
    )
    weight_bytes = 4 * width * width
    shape = jax.ShapeDtypeStruct
    two_weights = pltpu.VMEM((2, width, width), bf16)
    normed = pltpu.VMEM((max_len, width), bf16)

    def attention_block(layer, hidden, mods, branches):
        outs = [shape((max_len, width), bf16)]
        if branches:
            outs = [shape((max_len, width), f32)] + [shape((rows_own, width), bf16)] * 2
        arrays, places = stream.operands(3 * layer)
        results = kernel_call(
            functools.partial(attention_kernel, places, len(arrays), layer, heads, len(branches)),
            outs,
            [
                two_weights,
                normed,
                pltpu.VMEM((max_len, 3 * half), bf16),
                pltpu.VMEM((3 * heads, max_len, HDIM), bf16),
                pltpu.VMEM((max_len, half), bf16),
            ],
            [ids, hidden, mods, *branches],
            arrays,
            1,
            2 * max_len * width * 4 * half + 4 * max_len * max_len * half,
            weight_bytes,
            44 if branches else 60,
        )
        return results if branches else results[0]

    def both(partial):
        return [partial, exchange(partial, "tensor", 1)]

    def up_block(layer, hidden, mods, branches):
        arrays, places = stream.operands(3 * layer + 1)
        return kernel_call(
            functools.partial(up_kernel, places, len(arrays), layer),
            [shape((max_len, width), f32), shape((2, max_len, width), bf16)],
            [two_weights, normed],
            [ids, hidden, mods, *branches],
            arrays,
            1,
            4 * max_len * width * width,
            weight_bytes,
        )

    def down_block(layer, units):
        arrays, places = stream.operands(3 * layer + 2)
        return kernel_call(
            functools.partial(down_kernel, places, len(arrays)),
            shape((max_len, width), bf16),
            [two_weights],
            [ids, units],
            arrays,
            1,
            4 * max_len * width * width,
            weight_bytes,
        )

    def mlp_block(layer, own, hidden, mods, branches):
        arrays, places = stream.operands(3 * layer + 1)
        more_arrays, more_places = stream.operands(3 * layer + 2)
        counts = (len(arrays), len(more_arrays))
        return kernel_call(
            functools.partial(mlp_kernel, (places, more_places), counts, layer, own),
            [shape((rows_own, width), f32)] * own + [shape((rows_own, width), bf16)],
            [
                two_weights,
                two_weights,
                pltpu.VMEM((2, rows_own, width), bf16),
                pltpu.VMEM((rows_own, width), bf16),
            ],
            [ids, hidden, mods, *branches],
            arrays + more_arrays,
            2,
            8 * rows_own * width * width,
            2 * weight_bytes,
            60 if own else 44,
        )

    activated = jax.nn.silu(condition[0]).astype(bf16).reshape(-1, width_piece)
    stream.step()
    columns = lax.all_to_all(activated, "batch", 0, 0, tiled=True)
    stream.step(columns)
    sums = modulation_sums(columns, modulation_weight, final_modulation)
    mine = jnp.sum(lax.all_to_all(sums, "batch", 0, 0, tiled=True), axis=0)
    hidden = jnp.einsum(
        "pl,pd->ld", latents[0], embed_weight, precision=lax.Precision.HIGHEST
    ) + jnp.asarray(position_values(max_len, width))
    stream.step(mine, hidden)
    mods = all_columns(mine)
    stream.step(mods)
    partial = attention_block(0, hidden, mods, [])
    stream.step(partial)
    branches = both(partial)
    stream.step(branches)
    hidden, units = up_block(0, hidden, mods, branches)
    stream.step(units)
    branches = both(down_block(0, units))
    stream.step(branches)
    hidden, other_half, own_half = attention_block(1, hidden, mods, branches)
    stream.step(other_half, own_half)
    for_other = exchange(own_half, "tensor", 1)
    for_own = exchange(other_half, "tensor", 1)
    stream.step(for_other)
    (sent,) = mlp_block(1, False, hidden, mods, [other_half, for_other])
    theirs = exchange(sent, "tensor", 1)
    hidden, mine = mlp_block(1, True, hidden, mods, [own_half, for_own])
    hidden = hidden + mods[6 * layer_count - 1][None, :] * (
        mine.astype(f32) + theirs.astype(f32)
    )
    final_in = normalized(
        hidden, mods[6 * layer_count][None, :], mods[6 * layer_count + 1][None, :]
    ).astype(bf16)
    noise_own = lax.dot_general(
        output_weight, final_in, (((0,), (1,)), ((), ())), preferred_element_type=f32
    )[None]
    return finish(latents, lengths, timesteps, guidance, noise_own, rows_own)


def solution(mesh):
    in_specs = (
        P("batch", None, None),
        P("batch"),
        P("batch"),
        P("batch"),
        P("guide", "batch", None),
        P(),
        P(None, "batch", None, "tensor"),
        P("batch", None, "tensor"),
        P(None, "batch", None, "tensor"),
        P(None, "tensor", "batch"),
        P(None, "batch", "tensor"),
        P(None, "tensor", "batch"),
        P(),
    )
    out_specs = (P("batch", "guide", "tensor"), P("batch", "guide", "tensor"))
    sizes = mesh.shape
    small = sizes["batch"] == 8 and sizes["tensor"] == 2
    body = fast_local if small else local
    return jax.shard_map(body, mesh=mesh, in_specs=in_specs, out_specs=out_specs, check_vma=False)
```

```python
import functools
import math

import jax
import jax.numpy as jnp
import numpy as np
from jax import lax
from jax.experimental import pallas as pl
from jax.experimental.pallas import tpu as pltpu
from jax.sharding import PartitionSpec as P

HDIM = 72
TRAIN_STEPS = 1000
STRIDE = 20


norm_epsilon = 1e-06


def from_partner(block, axis, distance):
    count = lax.axis_size(axis)
    route = []
    for low in range(count):
        high = low | 1 << distance
        if high != low and high < count:
            route += [(low, high), (high, low)]
    return lax.ppermute(block, axis, route)


def layer_norm(values):
    center = values - jnp.mean(values, axis=-1, keepdims=True)
    spread = jnp.mean(center * center, axis=-1, keepdims=True)
    return center * lax.rsqrt(spread + norm_epsilon)


def modulate(values, shift, scale):
    return layer_norm(values) * (1.0 + scale[:, None, :]) + shift[:, None, :]


def position_values(row_count, width):
    half_width = width // 2
    frequency = np.exp(
        np.arange(half_width, dtype=np.float32) * np.float32(-math.log(10000.0) / half_width)
    )
    angles = np.arange(row_count, dtype=np.float32)[:, None] * frequency[None, :]
    return np.concatenate([np.sin(angles), np.cos(angles)], axis=1).astype(np.float32)


def position_table(row_count, width):
    rows_at = jnp.arange(row_count, dtype=jnp.int32).astype(jnp.float32)
    half_width = width // 2
    frequency = jnp.exp(
        jnp.arange(half_width, dtype=jnp.float32) * (-math.log(10000.0) / half_width)
    )
    angles = rows_at[:, None] * frequency[None, :]
    return jnp.concatenate([jnp.sin(angles), jnp.cos(angles)], axis=1)


def attend(operands):
    projected_item, key_live = operands
    score_scale = 1.0 / math.sqrt(HDIM)
    scores = (
        jnp.einsum(
            "qhd,khd->hqk",
            projected_item[:, 0],
            projected_item[:, 1],
            preferred_element_type=jnp.float32,
        )
        * score_scale
    )
    scores = jnp.where(key_live[None, None, :], scores, -jnp.inf)
    row_max = jnp.max(scores, axis=-1, keepdims=True)
    exp_scores = jnp.exp(scores - row_max)
    probabilities = (exp_scores / jnp.sum(exp_scores, axis=-1, keepdims=True)).astype(jnp.bfloat16)
    attended = jnp.einsum(
        "hqk,khd->qhd", probabilities, projected_item[:, 2], preferred_element_type=jnp.float32
    )
    return attended.astype(jnp.bfloat16).reshape(
        attended.shape[0], attended.shape[1] * attended.shape[2]
    )


def local(
    latents,
    lengths,
    timesteps,
    guidance,
    condition,
    embed_weight,
    modulation_weight,
    final_modulation,
    qkv_weight,
    proj_weight,
    up_weight,
    down_weight,
    output_weight,
):
    tensor_count = lax.axis_size("tensor")
    batch_count = lax.axis_size("batch")
    tensor_at = lax.axis_index("tensor")
    batch_at = lax.axis_index("batch")
    req_local, patch_size, max_len = latents.shape
    width = embed_weight.shape[1]
    layer_count = qkv_weight.shape[0]
    head_cols = qkv_weight.shape[3]
    heads_local = head_cols // HDIM
    rows_local = max_len // tensor_count
    width_piece = width // batch_count
    mod_count = 6 * layer_count + 2

    def rows_product(activation, shard):
        return jnp.dot(
            activation,
            lax.all_gather(shard, "batch", axis=0, tiled=True),
            preferred_element_type=jnp.float32,
        )

    def cols_product(activation, shard):
        return jnp.dot(
            activation,
            lax.all_gather(shard, "batch", axis=1, tiled=True),
            preferred_element_type=jnp.float32,
        )

    cond_act = jax.nn.silu(condition[0]).astype(jnp.bfloat16)
    cond_all = lax.all_gather(cond_act, "batch", axis=0, tiled=True)
    cond_cols = lax.dynamic_slice_in_dim(cond_all, batch_at * width_piece, width_piece, 1)
    block_local = jnp.transpose(modulation_weight, (1, 0, 2, 3)).reshape(
        width_piece, 6 * layer_count * head_cols
    )
    mod_local = jnp.concatenate(
        [block_local, final_modulation.reshape(width_piece, 2 * head_cols)], axis=1
    )
    mod_mine = lax.psum_scatter(
        jnp.dot(cond_cols, mod_local, preferred_element_type=jnp.float32),
        "batch",
        scatter_dimension=0,
        tiled=True,
    )
    mod_full = lax.all_gather(
        mod_mine.reshape(req_local, mod_count, head_cols), "tensor", axis=2, tiled=True
    )
    positions = jnp.arange(max_len, dtype=jnp.int32)
    live_mask = positions[None, :] < lengths[:, None]
    own_start = tensor_at * rows_local
    hidden_state = (
        jnp.einsum("rpl,pd->rld", latents, embed_weight, precision=lax.Precision.HIGHEST)
        + position_table(max_len, width)[None]
    )
    for layer_at in range(layer_count):
        modulation = mod_full[:, 6 * layer_at : 6 * layer_at + 6]
        normed = modulate(hidden_state, modulation[:, 0], modulation[:, 1]).astype(jnp.bfloat16)
        projected = rows_product(
            normed.reshape(req_local * max_len, width),
            qkv_weight[layer_at].reshape(width_piece, 3 * head_cols),
        ).astype(jnp.bfloat16)
        projected = projected.reshape(req_local, max_len, 3, heads_local, HDIM)
        attended = lax.map(attend, (projected, live_mask))
        branch = cols_product(
            attended.reshape(req_local * max_len, head_cols), proj_weight[layer_at]
        ).reshape(req_local, max_len, width)
        branch = lax.psum(branch.astype(jnp.bfloat16), "tensor").astype(jnp.float32)
        hidden_state = hidden_state + modulation[:, 2][:, None, :] * branch
        normed = modulate(hidden_state, modulation[:, 3], modulation[:, 4]).astype(jnp.bfloat16)
        hidden_units = jax.nn.gelu(
            rows_product(normed.reshape(req_local * max_len, width), up_weight[layer_at]),
            approximate=True,
        ).astype(jnp.bfloat16)
        branch = cols_product(hidden_units, down_weight[layer_at]).reshape(
            req_local, max_len, width
        )
        branch = lax.psum(branch.astype(jnp.bfloat16), "tensor").astype(jnp.float32)
        hidden_state = hidden_state + modulation[:, 5][:, None, :] * branch
    hidden_state = lax.dynamic_slice_in_dim(hidden_state, own_start, rows_local, 1)
    final_in = modulate(
        hidden_state, mod_full[:, 6 * layer_count], mod_full[:, 6 * layer_count + 1]
    ).astype(jnp.bfloat16)
    noise_own = jnp.einsum(
        "rld,dp->rpl", final_in, output_weight, preferred_element_type=jnp.float32
    )
    return finish(latents, lengths, timesteps, guidance, noise_own, rows_local)


def alpha_table():
    beta_values = np.linspace(0.0001, 0.02, TRAIN_STEPS, dtype=np.float32)
    return np.cumprod(np.float32(1.0) - beta_values, dtype=np.float32)


def finish(latents, lengths, timesteps, guidance, noise_own, rows_local):
    patch_size, max_len = latents.shape[1:]
    guide_at = lax.axis_index("guide")
    is_first = guide_at == 0
    own_start = lax.axis_index("tensor") * rows_local
    own_latents = lax.dynamic_slice_in_dim(latents, own_start, rows_local, 2)
    own_live = (own_start + jnp.arange(rows_local, dtype=jnp.int32))[None, :] < lengths[:, None]
    half_patch = patch_size // 2
    mine_noise = lax.dynamic_slice_in_dim(noise_own, guide_at * half_patch, half_patch, 1)
    other_noise = lax.dynamic_slice_in_dim(noise_own, (1 - guide_at) * half_patch, half_patch, 1)
    partner_noise = from_partner(other_noise, "guide", 0)
    cond_noise = jnp.where(is_first, mine_noise, partner_noise)
    uncond_noise = jnp.where(is_first, partner_noise, mine_noise)
    live_out = own_live[:, None, :]
    guided = uncond_noise + guidance[:, None, None] * (cond_noise - uncond_noise)
    guided = jnp.where(live_out, guided, 0.0)
    half_latents = lax.dynamic_slice_in_dim(own_latents, guide_at * half_patch, half_patch, 1)
    alpha_bar = jnp.asarray(alpha_table())
    step_ids = jnp.arange(TRAIN_STEPS, dtype=jnp.int32)
    alpha_now = jnp.sum(
        jnp.where(step_ids[None, :] == timesteps[:, None], alpha_bar[None, :], 0.0), axis=1
    )[:, None, None]
    alpha_prev = jnp.sum(
        jnp.where(step_ids[None, :] == (timesteps - STRIDE)[:, None], alpha_bar[None, :], 0.0),
        axis=1,
    )[:, None, None]
    start_est = (half_latents - jnp.sqrt(1.0 - alpha_now) * guided) / jnp.sqrt(alpha_now)
    previous = jnp.sqrt(alpha_prev) * start_est + jnp.sqrt(1.0 - alpha_prev) * guided
    previous = jnp.where(live_out, previous, 0.0)
    return (guided, previous)


def exchange(block, axis, bit):
    count = lax.axis_size(axis)
    return lax.ppermute(block, axis, [(at, at ^ bit) for at in range(count)])


HOLDS = {"own": (0,), "two": (4,), "pair": (0, 4), "four": (2, 6)}

PLAN = (
    ((("own", 0),), (("own", 0),)),
    ((("pair", 0),), (("two", 0), ("own", 1))),
    ((("own", 1),), (("four", 0),)),
    ((("pair", 1), ("own", 2)), (("two", 1), ("own", 2), ("own", 3))),
    ((("pair", 2), ("own", 3)), (("four", 1), ("two", 2))),
    ((("pair", 3), ("own", 4)), (("four", 2), ("two", 3))),
    ((("pair", 4), ("own", 5)), (("four", 3), ("pair", 4), ("own", 5))),
    ((("pair", 5),), (("four", 4), ("two", 5))),
    ((), (("four", 5),)),
)
READY = ((0,), (1, 2), (3,), (), (4, 5))


class Stream:
    def __init__(self, make_own):
        self.make_own, self.at = make_own, 0
        self.values, self.arrived, self.sent = {}, {}, ()
        self.blocks = [[] for _ in make_own]

    def hand_over(self, array, parts, flip):
        other = exchange(array, "guide", 1)
        at = 0
        for kind, piece in parts:
            for distance in HOLDS[kind]:
                for which, buffer in enumerate((array, other)):
                    self.blocks[piece].append((buffer, at, distance ^ flip, which))
                at += 1

    def step(self, *first):
        over_z, over_x = PLAN[self.at] if self.at < len(PLAN) else ((), ())
        for piece in READY[self.at] if self.at < len(READY) else ():
            self.values["own", piece] = self.make_own[piece]()
        self.at += 1
        self.values, arrived, _ = lax.optimization_barrier((self.values, self.arrived, first))
        self.values = values = dict(self.values)
        for (kind, piece), value in arrived.items():
            if kind == "own":
                values["two", piece] = value
                values["pair", piece] = jnp.concatenate([values["own", piece], value], axis=0)
            elif kind == "pair":
                values["four", piece] = value
        self.arrived = {}
        source = [values[part] for part in over_x]
        if source:
            source = source[0] if len(source) == 1 else jnp.concatenate(source, axis=0)
            self.arrived["x", ""] = exchange(source, "batch", 1)
        for kind, piece in over_z:
            bit = 4 if kind == "own" else 2
            self.arrived[kind, piece] = exchange(values[kind, piece], "batch", bit)
        if ("x", "") in arrived:
            self.hand_over(arrived["x", ""], self.sent, 1)
        if over_x:
            self.hand_over(source, over_x, 0)
        self.sent = over_x

    def operands(self, piece):
        arrays, places = [], []
        for buffer, at, distance, which in self.blocks[piece]:
            found = [n for n, array in enumerate(arrays) if array is buffer]
            if not found:
                arrays.append(buffer)
            places.append((found[0] if found else len(arrays) - 1, at, distance, which))
        return arrays, places


def fetch(weights, slots, buffers, places, batch_at, arrivals):
    rows = weights.shape[1] // (len(places) // 2)
    copies = []
    for number, (array, at, distance, which) in enumerate(sorted(places, key=lambda p: p[3])):
        row = pl.multiple_of((batch_at ^ distance) * rows, 16)
        copies.append(
            pltpu.make_async_copy(
                buffers[array].at[pl.ds(at * rows, rows), :],
                weights.at[slots[which], pl.ds(row, rows), :],
                arrivals.at[number],
            )
        )
        copies[-1].start()
    return copies


def normalized(hidden, shift, scale):
    center = hidden - jnp.mean(hidden, axis=-1, keepdims=True)
    spread = jnp.mean(center * center, axis=-1, keepdims=True)
    return center * lax.rsqrt(spread + norm_epsilon) * (1.0 + scale) + shift


def dot_nt(left, right):
    return lax.dot_general(
        left, right, (((1,), (1,)), ((), ())), preferred_element_type=jnp.float32
    )


def kernel_call(body, outs, scratch, operands, buffers, fetches, flops, bytes_moved, mib=44):
    specs = [pl.BlockSpec(memory_space=pltpu.SMEM)]
    specs += [pl.BlockSpec(memory_space=pltpu.VMEM) for _ in operands[1:]]
    specs += [pl.BlockSpec(memory_space=pl.ANY) for _ in buffers]
    scratch = scratch + [pltpu.SemaphoreType.DMA((16,))] * fetches
    return pl.pallas_call(
        body,
        out_shape=outs,
        in_specs=specs,
        out_specs=jax.tree.map(lambda _: pl.BlockSpec(memory_space=pltpu.VMEM), outs),
        scratch_shapes=scratch,
        cost_estimate=pl.CostEstimate(
            flops=int(flops), bytes_accessed=int(bytes_moved), transcendentals=0
        ),
        compiler_params=pltpu.CompilerParams(vmem_limit_bytes=mib * 2**20),
    )(*operands, *buffers)


def enter(hidden, branches, mods, row, hidden_out, normed, first_row=0):
    state = hidden[pl.ds(first_row, normed.shape[0]), :]
    if branches:
        total = branches[0][...].astype(jnp.float32) + branches[1][...].astype(jnp.float32)
        state = state + mods[row - 1 : row, :] * total
        if hidden_out is not None:
            hidden_out[...] = state
    normed[...] = normalized(state, mods[row : row + 1, :], mods[row + 1 : row + 2, :]).astype(
        jnp.bfloat16
    )


def attention_kernel(places, array_count, layer, heads, branch_count, ids, hidden, mods, *refs):
    branches, refs = refs[:branch_count], refs[branch_count:]
    buffers, refs = refs[:array_count], refs[array_count:]
    hidden_out = other_half = None
    if branches:
        hidden_out, other_half, refs = refs[0], refs[1], refs[2:]
    partial, weights, normed, projected, split, attended, arrivals = refs
    width, keys = hidden.shape[1], hidden.shape[0]
    half = width // 2
    copies = fetch(weights, [ids[1], 1 - ids[1]], buffers, places, ids[0], arrivals)
    enter(hidden, branches, mods, 6 * layer, hidden_out, normed)
    for copy in copies:
        copy.wait()

    def step(at, carry):
        lo = pl.multiple_of(at * 384, 128)
        projected[:, pl.ds(lo, 384)] = jnp.dot(
            normed[...], weights[0, :, pl.ds(lo, 384)], preferred_element_type=jnp.float32
        ).astype(jnp.bfloat16)
        return carry

    lax.fori_loop(0, width // 384, step, 0)
    projected[:, width:] = jnp.dot(
        normed[...], weights[1, :, :half], preferred_element_type=jnp.float32
    ).astype(jnp.bfloat16)
    for at in range(3 * heads):
        split[at] = projected[:, at * HDIM : (at + 1) * HDIM]
    factor = math.log2(math.e) / math.sqrt(HDIM)
    live = lax.broadcasted_iota(jnp.int32, (1, keys), 1) < ids[3]
    for at in range(heads):
        scores = dot_nt(split[at], split[heads + at])
        scores = jnp.where(live, scores * factor, -jnp.inf)
        raised = jnp.exp2(scores - jnp.max(scores, axis=-1, keepdims=True))
        total = jnp.sum(raised, axis=-1, keepdims=True)
        out = jnp.dot(
            raised.astype(jnp.bfloat16), split[2 * heads + at], preferred_element_type=jnp.float32
        )
        attended[:, at * HDIM : (at + 1) * HDIM] = (out / total).astype(jnp.bfloat16)
    proj = weights[1, :, half:]
    if other_half is None:
        partial[...] = dot_nt(attended[...], proj).astype(jnp.bfloat16)
    else:
        rows = partial.shape[0]
        for out, which in ((partial, ids[2]), (other_half, 1 - ids[2])):
            some = attended[pl.ds(pl.multiple_of(which * rows, 16), rows), :]
            out[...] = dot_nt(some, proj).astype(jnp.bfloat16)


def expand(normed, weights, units, copies):
    width, count = normed.shape[1], len(copies) // 2
    for half in range(2):
        for copy in copies[half * count : (half + 1) * count]:
            copy.wait()

        def step(at, carry):
            lo = pl.multiple_of(at * 384, 128)
            product = jnp.dot(
                normed[...], weights[half, :, pl.ds(lo, 384)], preferred_element_type=jnp.float32
            )
            inner = math.sqrt(2.0 / math.pi) * (product + 0.044715 * product * product * product)
            units[half, :, pl.ds(lo, 384)] = (0.5 * product * (1.0 + jnp.tanh(inner))).astype(
                jnp.bfloat16
            )
            return carry

        lax.fori_loop(0, width // 384, step, 0)


def contract(units, weights, partial):
    width = partial.shape[1]

    def step(at, carry):
        lo = pl.multiple_of(at * 384, 128)
        product = dot_nt(units[0], weights[0, pl.ds(lo, 384), :])
        product = product + dot_nt(units[1], weights[1, pl.ds(lo, 384), :])
        partial[:, pl.ds(lo, 384)] = product.astype(jnp.bfloat16)
        return carry

    lax.fori_loop(0, width // 384, step, 0)


def up_kernel(places, array_count, layer, ids, hidden, mods, *refs):
    branches, refs = refs[:2], refs[2:]
    buffers, refs = refs[:array_count], refs[array_count:]
    hidden_out, units, weights, normed, arrivals = refs
    copies = fetch(weights, [0, 1], buffers, places, ids[0], arrivals)
    enter(hidden, branches, mods, 6 * layer + 3, hidden_out, normed)
    expand(normed, weights, units, copies)


def down_kernel(places, array_count, ids, units, *refs):
    buffers, (partial, weights, arrivals) = refs[:array_count], refs[array_count:]
    for copy in fetch(weights, [0, 1], buffers, places, ids[0], arrivals):
        copy.wait()
    contract(units, weights, partial)


def mlp_kernel(places, counts, layer, own, ids, hidden, mods, *refs):
    branches, refs = refs[:2], refs[2:]
    ups, downs, refs = refs[: counts[0]], refs[counts[0] : sum(counts)], refs[sum(counts) :]
    hidden_out = None
    if own:
        hidden_out, refs = refs[0], refs[1:]
    partial, up_weights, down_weights, units, normed, arrivals, more_arrivals = refs
    rows = partial.shape[0]
    first_row = pl.multiple_of((ids[2] if own else 1 - ids[2]) * rows, 16)
    up_copies = fetch(up_weights, [0, 1], ups, places[0], ids[0], arrivals)
    down_copies = fetch(down_weights, [0, 1], downs, places[1], ids[0], more_arrivals)
    enter(hidden, branches, mods, 6 * layer + 3, hidden_out, normed, first_row)
    expand(normed, up_weights, units, up_copies)
    for copy in down_copies:
        copy.wait()
    contract(units, down_weights, partial)


def modulation_sums(columns, modulation_weight, final_modulation):
    layer_count, _, _, head_cols = modulation_weight.shape
    blocks = jnp.einsum(
        "rk,lkjc->rljc", columns, modulation_weight, preferred_element_type=jnp.float32
    ).reshape(columns.shape[0], 6 * layer_count, head_cols)
    finals = jnp.einsum("rk,kjc->rjc", columns, final_modulation, preferred_element_type=jnp.float32)
    return jnp.concatenate([blocks, finals], axis=1)


def all_columns(mine):
    other = exchange(mine, "tensor", 1)
    first = lax.axis_index("tensor") == 0
    return jnp.concatenate(
        [jnp.where(first, mine, other), jnp.where(first, other, mine)], axis=1
    )


def fast_local(
    latents,
    lengths,
    timesteps,
    guidance,
    condition,
    embed_weight,
    modulation_weight,
    final_modulation,
    qkv_weight,
    proj_weight,
    up_weight,
    down_weight,
    output_weight,
):
    tensor_at = lax.axis_index("tensor")
    batch_at = lax.axis_index("batch")
    guide_at = lax.axis_index("guide")
    _, patch_size, max_len = latents.shape
    width = embed_weight.shape[1]
    half = width // 2
    layer_count = qkv_weight.shape[0]
    heads = half // HDIM
    rows_own = max_len // 2
    width_piece = qkv_weight.shape[1]
    first = guide_at == 0
    ids = jnp.stack([batch_at, guide_at, tensor_at, lengths[0]]).astype(jnp.int32)
    bf16, f32 = jnp.bfloat16, jnp.float32

    def attention_piece(layer):
        queries_keys = qkv_weight[layer, :, :2].reshape(width_piece, width)
        values_proj = jnp.concatenate([qkv_weight[layer, :, 2], proj_weight[layer].T], axis=1)
        return jnp.where(first, queries_keys, values_proj)

    def up_piece(layer):
        return lax.dynamic_slice_in_dim(up_weight[layer], guide_at * width, width, 1)

    def down_piece(layer):
        return lax.dynamic_slice_in_dim(down_weight[layer], guide_at * width, width, 0).T

    stream = Stream(
        [
            functools.partial(make, layer)
            for layer in range(layer_count)
            for make in (attention_piece, up_piece, down_piece)
        ]
    )
    weight_bytes = 4 * width * width
    shape = jax.ShapeDtypeStruct
    two_weights = pltpu.VMEM((2, width, width), bf16)
    normed = pltpu.VMEM((max_len, width), bf16)

    def attention_block(layer, hidden, mods, branches):
        outs = [shape((max_len, width), bf16)]
        if branches:
            outs = [shape((max_len, width), f32)] + [shape((rows_own, width), bf16)] * 2
        arrays, places = stream.operands(3 * layer)
        results = kernel_call(
            functools.partial(attention_kernel, places, len(arrays), layer, heads, len(branches)),
            outs,
            [
                two_weights,
                normed,
                pltpu.VMEM((max_len, 3 * half), bf16),
                pltpu.VMEM((3 * heads, max_len, HDIM), bf16),
                pltpu.VMEM((max_len, half), bf16),
            ],
            [ids, hidden, mods, *branches],
            arrays,
            1,
            2 * max_len * width * 4 * half + 4 * max_len * max_len * half,
            weight_bytes,
            44 if branches else 60,
        )
        return results if branches else results[0]

    def both(partial):
        return [partial, exchange(partial, "tensor", 1)]

    def up_block(layer, hidden, mods, branches):
        arrays, places = stream.operands(3 * layer + 1)
        return kernel_call(
            functools.partial(up_kernel, places, len(arrays), layer),
            [shape((max_len, width), f32), shape((2, max_len, width), bf16)],
            [two_weights, normed],
            [ids, hidden, mods, *branches],
            arrays,
            1,
            4 * max_len * width * width,
            weight_bytes,
        )

    def down_block(layer, units):
        arrays, places = stream.operands(3 * layer + 2)
        return kernel_call(
            functools.partial(down_kernel, places, len(arrays)),
            shape((max_len, width), bf16),
            [two_weights],
            [ids, units],
            arrays,
            1,
            4 * max_len * width * width,
            weight_bytes,
        )

    def mlp_block(layer, own, hidden, mods, branches):
        arrays, places = stream.operands(3 * layer + 1)
        more_arrays, more_places = stream.operands(3 * layer + 2)
        counts = (len(arrays), len(more_arrays))
        return kernel_call(
            functools.partial(mlp_kernel, (places, more_places), counts, layer, own),
            [shape((rows_own, width), f32)] * own + [shape((rows_own, width), bf16)],
            [
                two_weights,
                two_weights,
                pltpu.VMEM((2, rows_own, width), bf16),
                pltpu.VMEM((rows_own, width), bf16),
            ],
            [ids, hidden, mods, *branches],
            arrays + more_arrays,
            2,
            8 * rows_own * width * width,
            2 * weight_bytes,
            60 if own else 44,
        )

    activated = jax.nn.silu(condition[0]).astype(bf16).reshape(-1, width_piece)
    stream.step()
    columns = lax.all_to_all(activated, "batch", 0, 0, tiled=True)
    stream.step(columns)
    sums = modulation_sums(columns, modulation_weight, final_modulation)
    mine = jnp.sum(lax.all_to_all(sums, "batch", 0, 0, tiled=True), axis=0)
    hidden = jnp.einsum(
        "pl,pd->ld", latents[0], embed_weight, precision=lax.Precision.HIGHEST
    ) + jnp.asarray(position_values(max_len, width))
    stream.step(mine, hidden)
    mods = all_columns(mine)
    stream.step(mods)
    partial = attention_block(0, hidden, mods, [])
    stream.step(partial)
    branches = both(partial)
    stream.step(branches)
    hidden, units = up_block(0, hidden, mods, branches)
    stream.step(units)
    branches = both(down_block(0, units))
    stream.step(branches)
    hidden, other_half, own_half = attention_block(1, hidden, mods, branches)
    stream.step(other_half, own_half)
    for_other = exchange(own_half, "tensor", 1)
    for_own = exchange(other_half, "tensor", 1)
    stream.step(for_other)
    (sent,) = mlp_block(1, False, hidden, mods, [other_half, for_other])
    theirs = exchange(sent, "tensor", 1)
    hidden, mine = mlp_block(1, True, hidden, mods, [own_half, for_own])
    hidden = hidden + mods[6 * layer_count - 1][None, :] * (
        mine.astype(f32) + theirs.astype(f32)
    )
    final_in = normalized(
        hidden, mods[6 * layer_count][None, :], mods[6 * layer_count + 1][None, :]
    ).astype(bf16)
    noise_own = lax.dot_general(
        output_weight, final_in, (((0,), (1,)), ((), ())), preferred_element_type=f32
    )[None]
    return finish(latents, lengths, timesteps, guidance, noise_own, rows_own)


def solution(mesh):
    in_specs = (
        P("batch", None, None),
        P("batch"),
        P("batch"),
        P("batch"),
        P("guide", "batch", None),
        P(),
        P(None, "batch", None, "tensor"),
        P("batch", None, "tensor"),
        P(None, "batch", None, "tensor"),
        P(None, "tensor", "batch"),
        P(None, "batch", "tensor"),
        P(None, "tensor", "batch"),
        P(),
    )
    out_specs = (P("batch", "guide", "tensor"), P("batch", "guide", "tensor"))
    sizes = mesh.shape
    small = sizes["batch"] == 8 and sizes["tensor"] == 2
    body = fast_local if small else local
    return jax.shard_map(body, mesh=mesh, in_specs=in_specs, out_specs=out_specs, check_vma=False)
```
